128 devices in a mesh: slide: 32 (over y_lo, x, z), region: 4 (over y_hi, core).
Axes of the slice: x: 4, y: 4 (y_hi: 2, y_lo: 2; y = y_hi * 2 + y_lo), z: 4, core: 2. Of those that a mesh axis runs over, the one named last changes fastest.
Arguments:
- tiles: bfloat16 [32, 4, 32, 196, 1024], P('slide', 'region'), may hold values from -6 to 6
- counts: int32 [32, 4], P('slide', 'region'), may hold values from 1 to 31, as said below
- tissue_mask: int32 [32, 4, 32, 196], P('slide', 'region'), may hold values 0 or 1
- w_reduce: bfloat16 [2, 1024, 256], replicated, may hold values from -0.1875 to 0.1875
- b_reduce: float32 [2, 256], replicated, may hold values from -3 to 3
- w_spatial: bfloat16 [2, 9, 256, 256], replicated, may hold values from -0.125 to 0.125
- b_spatial: float32 [2, 256], replicated, may hold values from -3 to 3
- w_expand: bfloat16 [2, 256, 1024], replicated, may hold values from -0.375 to 0.375
- proj_w: bfloat16 [1024, 256], replicated, may hold values from -0.1875 to 0.1875
Outputs:
- embedded: float32 [32, 4, 32, 196, 256], P('slide', 'region')
The draws below stay inside these ranges and needn't reach their ends.
Inputs may be any that keep to these rules, and one draw needn't show every extreme that they name: For each region, the counts of slide s and slide s + 16 add up to at most 32.
All inputs are finite; a program needn't handle non-finite values. No bound on the sum of `tissue_mask` on one device may be relied on, other than what follows from the above.
Results may differ from the reference program's by a relative error of at most 0.0022.
Values may be sent and summed in bfloat16 or wider, within the bound.
A program may use at most 192 MiB of HBM per device.

```python
import jax
import jax.numpy as jnp
from jax import lax

CHAN = 1024
MID = 256
EMB = 256
TILE = 14
BLOCKS = 2
TCOLS = 4
MAXT = 32
CELLS = 196
TROWS = 8
SLIDES = 32
REGIONS = 4


def draw_counts(key, part):
    key_heavy, key_light, key_flip = jax.random.split(key, 3)
    paired = SLIDES // 2
    heavy = jax.random.randint(key_heavy, (paired, REGIONS), MAXT // 2 + 1, MAXT)
    spread = jax.random.randint(key_light, (paired, REGIONS), 0, 1 << 20)
    light = spread % (MAXT - heavy) + 1
    heavy = heavy.at[0, 0].set(MAXT - 1)
    light = light.at[0, 0].set(1)
    flipped = jax.random.randint(key_flip, (paired, REGIONS), 0, 2) == 1
    upper = jnp.where(flipped, heavy, light)
    lower = jnp.where(flipped, light, heavy)
    return jnp.concatenate([upper, lower], 0).astype(jnp.int32)


def plant(values, key, low, largest):
    longest = values.shape.index(max(values.shape))
    spots = []
    for shift in (0, 1):
        where = [jax.random.randint(jax.random.fold_in(key, axis), (), 0, length) for axis, length in enumerate(values.shape)]
        where[longest] = (where[longest] + shift) % values.shape[longest]
        spots.append(tuple(where))
    return values.at[spots[0]].set(low).at[spots[1]].set(largest)


def block_scale(rng, extent, pieces, smallest, largest):
    def one(axis_at, shards_of):
        draws = jax.random.uniform(jax.random.fold_in(jax.random.fold_in(rng, 6), axis_at), (shards_of,), jnp.float32, smallest / len(pieces), largest / len(pieces))
        return jnp.repeat(jnp.exp(draws), extent[axis_at] // shards_of).reshape((-1,) + (1,) * (len(extent) - axis_at - 1))

    level = one(*pieces[0])
    for cut in pieces[1:]:
        level = level * one(*cut)
    return level


def scatter_about(own_key, dims, scale, limit, cuts=(), kind=jnp.bfloat16):
    drawn = jax.random.normal(own_key, dims, jnp.float32) * scale
    if len(cuts) > 0:
        drawn = block_scale(own_key, dims, cuts, -0.22, 0.18) * drawn
    return jnp.clip(drawn, min=-limit, max=limit).astype(kind)


def setup_inputs(seed: int = 0) -> dict:
    key_list = jax.random.split(jax.random.key(seed), 10)
    tiles = scatter_about(key_list[0], (SLIDES, REGIONS, MAXT, CELLS, CHAN), 1.0, 6.0, ((0, 32), (1, 4)))
    counts = draw_counts(jax.random.fold_in(key_list[9], 71), 0)
    tissue_mask = plant((jax.random.randint(key_list[2], (SLIDES, REGIONS, MAXT, CELLS), 0, 4) < 3).astype(jnp.int32), jax.random.fold_in(key_list[2], 1), 0, 1)
    w_reduce = scatter_about(key_list[3], (BLOCKS, CHAN, MID), CHAN ** -0.5, 0.1875)
    b_reduce = scatter_about(key_list[4], (BLOCKS, MID), 0.5, 3.0, (), jnp.float32)
    w_spatial = scatter_about(key_list[5], (BLOCKS, 9, MID, MID), (9 * MID) ** -0.5, 0.125)
    b_spatial = scatter_about(key_list[6], (BLOCKS, MID), 0.5, 3.0, (), jnp.float32)
    w_expand = scatter_about(key_list[7], (BLOCKS, MID, CHAN), MID ** -0.5, 0.375)
    proj_w = scatter_about(key_list[8], (CHAN, EMB), CHAN ** -0.5, 0.1875)
    return dict(tiles=tiles, counts=counts, tissue_mask=tissue_mask, w_reduce=w_reduce, b_reduce=b_reduce, w_spatial=w_spatial, b_spatial=b_spatial, w_expand=w_expand, proj_w=proj_w)


def features(tiles_in, w_reduce, b_reduce, w_spatial, b_spatial, w_expand):
    tile_count = tiles_in.shape[0]
    current = tiles_in
    for section_idx in range(BLOCKS):
        flat_in = current.reshape(-1, CHAN)
        reduced = jax.nn.relu(jnp.dot(flat_in, w_reduce[section_idx], preferred_element_type=jnp.float32) + b_reduce[section_idx]).astype(jnp.bfloat16)
        padded = jnp.pad(reduced.reshape(tile_count, TILE, TILE, MID), ((0, 0), (1, 1), (1, 1), (0, 0)))
        summed = jnp.zeros((tile_count * TILE * TILE, MID), jnp.float32)
        for row_off in range(3):
            for col_off in range(3):
                window = padded[:, row_off:row_off + TILE, col_off:col_off + TILE, :].reshape(-1, MID)
                summed = summed + jnp.dot(window, w_spatial[section_idx, 3 * row_off + col_off], preferred_element_type=jnp.float32)
        spatial = jax.nn.relu(summed + b_spatial[section_idx]).astype(jnp.bfloat16)
        expanded = jnp.dot(spatial, w_expand[section_idx], preferred_element_type=jnp.float32)
        current = jax.nn.relu(flat_in.astype(jnp.float32) + expanded).astype(jnp.bfloat16).reshape(tile_count, TILE, TILE, CHAN)
    return current


def reference(tiles, counts, tissue_mask, w_reduce, b_reduce, w_spatial, b_spatial, w_expand, proj_w):
    flat_tiles = tiles.reshape(SLIDES * REGIONS, MAXT, TILE, TILE, CHAN)
    flat_counts = counts.reshape(SLIDES * REGIONS)
    flat_mask = tissue_mask.reshape(SLIDES * REGIONS, MAXT, CELLS)

    def one_region(packed):
        region_tiles, region_count, region_mask = packed
        mapped = features(region_tiles, w_reduce, b_reduce, w_spatial, b_spatial, w_expand)
        projected = jnp.dot(mapped.reshape(-1, CHAN), proj_w, preferred_element_type=jnp.float32).reshape(MAXT, CELLS, EMB)
        alive = jnp.arange(MAXT, dtype=jnp.int32) < region_count
        weight = jnp.where(alive[:, None], region_mask, 0).astype(jnp.float32)
        return projected * weight[:, :, None]

    weighted = lax.map(one_region, (flat_tiles, flat_counts, flat_mask))
    image = weighted.reshape(SLIDES, REGIONS, TROWS, TCOLS, TILE, TILE, EMB).transpose(0, 1, 2, 4, 3, 5, 6)
    image = image.reshape(SLIDES, REGIONS * TROWS * TILE, TCOLS * TILE, EMB)
    height = REGIONS * TROWS * TILE
    width = TCOLS * TILE
    framed = jnp.pad(image, ((0, 0), (1, 1), (1, 1), (0, 0)))
    total = jnp.zeros_like(image)
    for row_off in range(3):
        for col_off in range(3):
            total = total + framed[:, row_off:row_off + height, col_off:col_off + width, :]
    averaged = total / 9.0
    averaged = averaged.reshape(SLIDES, REGIONS, TROWS, TILE, TCOLS, TILE, EMB).transpose(0, 1, 2, 4, 3, 5, 6)
    return averaged.reshape(SLIDES, REGIONS, MAXT, CELLS, EMB)
```

```python
import jax
import jax.numpy as jnp
from jax import lax
from jax.sharding import PartitionSpec as P

CHAN = 1024
MID = 256
TILE = 14
BLOCKS = 2
TCOLS = 4


def swapped(block, axis, stride):
    count = lax.axis_size(axis)
    route = []
    for low in range(count):
        high = low | 1 << stride
        if high != low and high < count:
            route += [(low, high), (high, low)]
    return lax.ppermute(block, axis, route)


def with_halo(block, sides, width):
    for axis, dim in sides:
        count = lax.axis_size(axis)
        forward = [(i, i + 1) for i in range(count - 1)]
        backward = [(target, source) for source, target in forward]
        low = lax.ppermute(
            lax.slice_in_dim(block, block.shape[dim] - width, None, axis=dim), axis, forward
        )
        high = lax.ppermute(lax.slice_in_dim(block, 0, width, axis=dim), axis, backward)
        block = jnp.concatenate([low, block, high], axis=dim)
    return block


def features(tiles_in, w_reduce, b_reduce, w_spatial, b_spatial, w_expand):
    tile_count = tiles_in.shape[0]
    current = tiles_in
    for section_idx in range(BLOCKS):
        flat_in = current.reshape(-1, CHAN)
        reduced = jax.nn.relu(
            jnp.dot(flat_in, w_reduce[section_idx], preferred_element_type=jnp.float32)
            + b_reduce[section_idx]
        ).astype(jnp.bfloat16)
        kernel = w_spatial[section_idx].reshape(3, 3, MID, MID)
        summed = lax.conv_general_dilated(
            reduced.reshape(tile_count, TILE, TILE, MID),
            kernel,
            (1, 1),
            ((1, 1), (1, 1)),
            dimension_numbers=("NHWC", "HWIO", "NHWC"),
            preferred_element_type=jnp.float32,
        ).reshape(-1, MID)
        spatial = jax.nn.relu(summed + b_spatial[section_idx]).astype(jnp.bfloat16)
        expanded = jnp.dot(spatial, w_expand[section_idx], preferred_element_type=jnp.float32)
        current = (
            jax.nn.relu(flat_in.astype(jnp.float32) + expanded)
            .astype(jnp.bfloat16)
            .reshape(tile_count, TILE, TILE, CHAN)
        )
    return current


def project(mapped, proj_w):
    return jnp.dot(mapped.reshape(-1, CHAN), proj_w, preferred_element_type=jnp.float32).reshape(
        mapped.shape[0], TILE * TILE, -1
    )


def per_device(
    tiles, counts, tissue_mask, w_reduce, b_reduce, w_spatial, b_spatial, w_expand, proj_w
):
    slots = tiles.shape[2]
    held = counts[0, 0]
    positions = jnp.arange(slots, dtype=jnp.int32)
    alive = positions < held
    local_tiles = tiles[0, 0].reshape(slots, TILE, TILE, CHAN)
    computed = features(local_tiles, w_reduce, b_reduce, w_spatial, b_spatial, w_expand)
    projected = project(computed, proj_w)
    weight = jnp.where(alive[:, None], tissue_mask[0, 0], 0).astype(jnp.float32)
    weighted = projected * weight[:, :, None]
    tile_rows = slots // TCOLS
    image = weighted.reshape(tile_rows, TCOLS, TILE, TILE, -1).transpose(0, 2, 1, 3, 4)
    image = image.reshape(tile_rows * TILE, TCOLS * TILE, -1)
    height = image.shape[0]
    width = image.shape[1]
    extended = with_halo(image, (("region", 0),), 1)
    framed = jnp.pad(extended, ((0, 0), (1, 1), (0, 0)))
    total = jnp.zeros_like(image)
    for row_off in range(3):
        for col_off in range(3):
            total = total + framed[row_off : row_off + height, col_off : col_off + width, :]
    averaged = total / 9.0
    averaged = averaged.reshape(tile_rows, TILE, TCOLS, TILE, -1).transpose(0, 2, 1, 3, 4)
    return averaged.reshape(1, 1, slots, TILE * TILE, -1)


def solution(mesh):
    placed = (
        P("slide", "region", None, None, None),
        P("slide", "region"),
        P("slide", "region", None, None),
        P(),
        P(),
        P(),
        P(),
        P(),
        P(),
    )
    return jax.shard_map(
        per_device,
        mesh=mesh,
        in_specs=placed,
        out_specs=P("slide", "region", None, None, None),
        check_vma=False,
    )
```

```python
import jax
import jax.numpy as jnp
from jax import lax
from jax.experimental import pallas as pl
from jax.experimental.pallas import tpu as pltpu
from jax.sharding import PartitionSpec as P

CHAN = 1024
MID = 256
TILE = 14
BLOCKS = 2
TCOLS = 4
CELLS = TILE * TILE
WIDE = 16
PADDED = TILE * WIDE


def tile_kernel(
    count_ref, x_ref, m_ref, wr_ref, br_ref, ws_ref, bs_ref, we_ref, pw_ref, o_ref,
    cur_ref, r_ref, s_ref, c_ref, q_ref,
):
    t = pl.program_id(0)

    @pl.when(t >= count_ref[0])
    def _():
        o_ref[...] = jnp.zeros(o_ref.shape, o_ref.dtype)

    @pl.when(t < count_ref[0])
    def _():
        s_ref[...] = jnp.zeros(s_ref.shape, s_ref.dtype)
        c_ref[0:WIDE, :] = jnp.zeros((WIDE, 3 * MID), jnp.bfloat16)
        c_ref[WIDE + PADDED:, :] = jnp.zeros((WIDE, 3 * MID), jnp.bfloat16)
        cur_ref[...] = x_ref[0]
        for b in range(BLOCKS):
            x = cur_ref[...]
            r = jnp.dot(x, wr_ref[b], preferred_element_type=jnp.float32) + br_ref[b]
            r_ref[...] = jnp.maximum(r, 0.0)
            for i in range(TILE):
                s_ref[pl.ds(8 + WIDE * i, TILE), :] = r_ref[pl.ds(TILE * i, TILE), :]
            c_ref[WIDE : WIDE + PADDED, 0:MID] = s_ref[pl.ds(7, PADDED), :].astype(jnp.bfloat16)
            c_ref[WIDE : WIDE + PADDED, MID : 2 * MID] = s_ref[pl.ds(8, PADDED), :].astype(jnp.bfloat16)
            c_ref[WIDE : WIDE + PADDED, 2 * MID :] = s_ref[pl.ds(9, PADDED), :].astype(jnp.bfloat16)
            acc = jnp.dot(c_ref[0:PADDED, :], ws_ref[b, 0], preferred_element_type=jnp.float32)
            acc += jnp.dot(c_ref[WIDE : WIDE + PADDED, :], ws_ref[b, 1], preferred_element_type=jnp.float32)
            acc += jnp.dot(c_ref[2 * WIDE : 2 * WIDE + PADDED, :], ws_ref[b, 2], preferred_element_type=jnp.float32)
            q_ref[...] = jnp.maximum(acc + bs_ref[b], 0.0)
            for i in range(TILE):
                r_ref[pl.ds(TILE * i, TILE), :] = q_ref[pl.ds(WIDE * i, TILE), :]
            spatial = r_ref[...].astype(jnp.bfloat16)
            e = jnp.dot(spatial, we_ref[b], preferred_element_type=jnp.float32)
            cur_ref[...] = jnp.maximum(x.astype(jnp.float32) + e, 0.0).astype(jnp.bfloat16)
        proj = jnp.dot(cur_ref[...], pw_ref[...], preferred_element_type=jnp.float32)
        o_ref[0] = proj * m_ref[0]


def tile_features(count, x, weight, w_reduce, b_reduce, w_spatial, b_spatial, w_expand, proj_w):
    slots = x.shape[0]
    emb = proj_w.shape[1]
    ws = w_spatial.reshape(BLOCKS, 3, 3 * MID, MID)
    br = b_reduce.reshape(BLOCKS, 1, MID)
    bs = b_spatial.reshape(BLOCKS, 1, MID)

    def live(t, c):
        return (jnp.maximum(jnp.minimum(t, c[0] - 1), 0), 0, 0)

    def whole(nd):
        return lambda t, c: (0,) * nd

    grid_spec = pltpu.PrefetchScalarGridSpec(
        num_scalar_prefetch=1,
        grid=(slots,),
        in_specs=[
            pl.BlockSpec((1, CELLS, CHAN), live),
            pl.BlockSpec((1, CELLS, 1), lambda t, c: (t, 0, 0)),
            pl.BlockSpec((BLOCKS, CHAN, MID), whole(3)),
            pl.BlockSpec((BLOCKS, 1, MID), whole(3)),
            pl.BlockSpec((BLOCKS, 3, 3 * MID, MID), whole(4)),
            pl.BlockSpec((BLOCKS, 1, MID), whole(3)),
            pl.BlockSpec((BLOCKS, MID, CHAN), whole(3)),
            pl.BlockSpec((CHAN, emb), whole(2)),
        ],
        out_specs=pl.BlockSpec((1, CELLS, emb), lambda t, c: (t, 0, 0)),
        scratch_shapes=[
            pltpu.VMEM((CELLS, CHAN), jnp.bfloat16),
            pltpu.VMEM((CELLS, MID), jnp.float32),
            pltpu.VMEM((PADDED + WIDE, MID), jnp.float32),
            pltpu.VMEM((PADDED + 2 * WIDE, 3 * MID), jnp.bfloat16),
            pltpu.VMEM((PADDED, MID), jnp.float32),
        ],
    )
    flops = 2 * slots * CELLS * (BLOCKS * (2 * CHAN * MID + 9 * MID * MID) + CHAN * emb)
    return pl.pallas_call(
        tile_kernel,
        grid_spec=grid_spec,
        out_shape=jax.ShapeDtypeStruct((slots, CELLS, emb), jnp.float32),
        compiler_params=pltpu.CompilerParams(
            dimension_semantics=("arbitrary",), vmem_limit_bytes=48 * 1024 * 1024
        ),
        cost_estimate=pl.CostEstimate(
            flops=flops, transcendentals=0, bytes_accessed=slots * CELLS * (2 * CHAN + 4 * emb + 4)
        ),
    )(count, x, weight, w_reduce, br, ws, bs, w_expand, proj_w)


def with_halo(block, sides, width):
    for axis, dim in sides:
        count = lax.axis_size(axis)
        forward = [(i, i + 1) for i in range(count - 1)]
        backward = [(target, source) for source, target in forward]
        low = lax.ppermute(
            lax.slice_in_dim(block, block.shape[dim] - width, None, axis=dim), axis, forward
        )
        high = lax.ppermute(lax.slice_in_dim(block, 0, width, axis=dim), axis, backward)
        block = jnp.concatenate([low, block, high], axis=dim)
    return block


def per_device(
    tiles, counts, tissue_mask, w_reduce, b_reduce, w_spatial, b_spatial, w_expand, proj_w
):
    slots = tiles.shape[2]
    held = counts[0]
    positions = jnp.arange(slots, dtype=jnp.int32)
    alive = positions < held[0]
    weight = jnp.where(alive[:, None], tissue_mask[0, 0], 0).astype(jnp.float32)
    weighted = tile_features(
        held, tiles[0, 0], weight[:, :, None], w_reduce, b_reduce, w_spatial, b_spatial, w_expand, proj_w
    )
    tile_rows = slots // TCOLS
    image = weighted.reshape(tile_rows, TCOLS, TILE, TILE, -1).transpose(0, 2, 1, 3, 4)
    image = image.reshape(tile_rows * TILE, TCOLS * TILE, -1)
    height = image.shape[0]
    width = image.shape[1]
    extended = with_halo(image, (("region", 0),), 1)
    framed = jnp.pad(extended, ((0, 0), (1, 1), (0, 0)))
    total = jnp.zeros_like(image)
    for row_off in range(3):
        for col_off in range(3):
            total = total + framed[row_off : row_off + height, col_off : col_off + width, :]
    averaged = total / 9.0
    averaged = averaged.reshape(tile_rows, TILE, TCOLS, TILE, -1).transpose(0, 2, 1, 3, 4)
    return averaged.reshape(1, 1, slots, TILE * TILE, -1)


def solution(mesh):
    placed = (
        P("slide", "region", None, None, None),
        P("slide", "region"),
        P("slide", "region", None, None),
        P(),
        P(),
        P(),
        P(),
        P(),
        P(),
    )
    return jax.shard_map(
        per_device,
        mesh=mesh,
        in_specs=placed,
        out_specs=P("slide", "region", None, None, None),
        check_vma=False,
    )
```

```python
import jax
import jax.numpy as jnp
from jax import lax
from jax.experimental import pallas as pl
from jax.experimental.pallas import tpu as pltpu
from jax.sharding import PartitionSpec as P

CHAN = 1024
MID = 256
TILE = 14
BLOCKS = 2
TCOLS = 4
CELLS = TILE * TILE
WIDE = 16
PADDED = TILE * WIDE


def tile_kernel(
    count_ref, x_ref, m_ref, wr_ref, br_ref, ws_ref, bs_ref, we_ref, pw_ref, o_ref,
    cur_ref, r_ref, s_ref, c_ref, q_ref,
):
    t = pl.program_id(0)

    @pl.when(t >= count_ref[0])
    def _():
        o_ref[...] = jnp.zeros(o_ref.shape, o_ref.dtype)

    @pl.when(t < count_ref[0])
    def _():
        s_ref[...] = jnp.zeros(s_ref.shape, s_ref.dtype)
        c_ref[0:WIDE, :] = jnp.zeros((WIDE, 3 * MID), jnp.bfloat16)
        c_ref[WIDE + PADDED:, :] = jnp.zeros((WIDE, 3 * MID), jnp.bfloat16)
        cur_ref[...] = x_ref[0]
        for b in range(BLOCKS):
            x = cur_ref[...]
            r = jnp.dot(x, wr_ref[b], preferred_element_type=jnp.float32) + br_ref[b]
            r_ref[...] = jnp.maximum(r, 0.0)
            for i in range(TILE):
                s_ref[pl.ds(8 + WIDE * i, TILE), :] = r_ref[pl.ds(TILE * i, TILE), :]
            c_ref[WIDE : WIDE + PADDED, 0:MID] = s_ref[pl.ds(7, PADDED), :].astype(jnp.bfloat16)
            c_ref[WIDE : WIDE + PADDED, MID : 2 * MID] = s_ref[pl.ds(8, PADDED), :].astype(jnp.bfloat16)
            c_ref[WIDE : WIDE + PADDED, 2 * MID :] = s_ref[pl.ds(9, PADDED), :].astype(jnp.bfloat16)
            acc = jnp.dot(c_ref[0:PADDED, :], ws_ref[b, 0], preferred_element_type=jnp.float32)
            acc += jnp.dot(c_ref[WIDE : WIDE + PADDED, :], ws_ref[b, 1], preferred_element_type=jnp.float32)
            acc += jnp.dot(c_ref[2 * WIDE : 2 * WIDE + PADDED, :], ws_ref[b, 2], preferred_element_type=jnp.float32)
            q_ref[...] = jnp.maximum(acc + bs_ref[b], 0.0)
            for i in range(TILE):
                r_ref[pl.ds(TILE * i, TILE), :] = q_ref[pl.ds(WIDE * i, TILE), :]
            spatial = r_ref[...].astype(jnp.bfloat16)
            e = jnp.dot(spatial, we_ref[b], preferred_element_type=jnp.float32)
            cur_ref[...] = jnp.maximum(x.astype(jnp.float32) + e, 0.0).astype(jnp.bfloat16)
        proj = jnp.dot(cur_ref[...], pw_ref[...], preferred_element_type=jnp.float32)
        o_ref[0] = proj * m_ref[0]


def tile_features(count, x, weight, w_reduce, b_reduce, w_spatial, b_spatial, w_expand, proj_w):
    slots = x.shape[0]
    emb = proj_w.shape[1]
    ws = w_spatial.reshape(BLOCKS, 3, 3 * MID, MID)
    br = b_reduce.reshape(BLOCKS, 1, MID)
    bs = b_spatial.reshape(BLOCKS, 1, MID)

    def live(t, c):
        return (jnp.maximum(jnp.minimum(t, c[0] - 1), 0), 0, 0)

    def whole(nd):
        return lambda t, c: (0,) * nd

    grid_spec = pltpu.PrefetchScalarGridSpec(
        num_scalar_prefetch=1,
        grid=(slots,),
        in_specs=[
            pl.BlockSpec((1, CELLS, CHAN), live),
            pl.BlockSpec((1, CELLS, 1), lambda t, c: (t, 0, 0)),
            pl.BlockSpec((BLOCKS, CHAN, MID), whole(3)),
            pl.BlockSpec((BLOCKS, 1, MID), whole(3)),
            pl.BlockSpec((BLOCKS, 3, 3 * MID, MID), whole(4)),
            pl.BlockSpec((BLOCKS, 1, MID), whole(3)),
            pl.BlockSpec((BLOCKS, MID, CHAN), whole(3)),
            pl.BlockSpec((CHAN, emb), whole(2)),
        ],
        out_specs=pl.BlockSpec((1, CELLS, emb), lambda t, c: (t, 0, 0)),
        scratch_shapes=[
            pltpu.VMEM((CELLS, CHAN), jnp.bfloat16),
            pltpu.VMEM((CELLS, MID), jnp.float32),
            pltpu.VMEM((PADDED + WIDE, MID), jnp.float32),
            pltpu.VMEM((PADDED + 2 * WIDE, 3 * MID), jnp.bfloat16),
            pltpu.VMEM((PADDED, MID), jnp.float32),
        ],
    )
    flops = 2 * slots * CELLS * (BLOCKS * (2 * CHAN * MID + 9 * MID * MID) + CHAN * emb)
    return pl.pallas_call(
        tile_kernel,
        grid_spec=grid_spec,
        out_shape=jax.ShapeDtypeStruct((slots, CELLS, emb), jnp.float32),
        compiler_params=pltpu.CompilerParams(
            dimension_semantics=("arbitrary",), vmem_limit_bytes=48 * 1024 * 1024
        ),
        cost_estimate=pl.CostEstimate(
            flops=flops, transcendentals=0, bytes_accessed=slots * CELLS * (2 * CHAN + 4 * emb + 4)
        ),
    )(count, x, weight, w_reduce, br, ws, bs, w_expand, proj_w)


GUARD = 16


def box_kernel(w_ref, hu_ref, hd_ref, j_ref, o_ref, g_ref, v_ref):
    tr = pl.program_id(0)
    rows = pl.num_programs(0)
    col = j_ref[...]
    for tc in range(TCOLS):
        t = tr * TCOLS + tc
        g_ref[TILE : TILE + CELLS, :] = w_ref[t]

        @pl.when(tr == 0)
        def _():
            g_ref[0:TILE, :] = hu_ref[tc]

        @pl.when(tr > 0)
        def _():
            g_ref[0:TILE, :] = w_ref[t - TCOLS, CELLS - TILE : CELLS, :]

        @pl.when(tr == rows - 1)
        def _():
            g_ref[TILE + CELLS : 2 * TILE + CELLS, :] = hd_ref[tc]

        @pl.when(tr < rows - 1)
        def _():
            g_ref[TILE + CELLS : 2 * TILE + CELLS, :] = w_ref[t + TCOLS, 0:TILE, :]

        v = g_ref[0:CELLS, :] + g_ref[TILE : TILE + CELLS, :] + g_ref[2 * TILE : 2 * TILE + CELLS, :]
        v_ref[tc, GUARD : GUARD + CELLS, :] = v
    for tc in range(TCOLS):
        h = v_ref[tc, GUARD : GUARD + CELLS, :]
        h = h + jnp.where(col != 0, v_ref[tc, GUARD - 1 : GUARD - 1 + CELLS, :], 0.0)
        h = h + jnp.where(col != TILE - 1, v_ref[tc, GUARD + 1 : GUARD + 1 + CELLS, :], 0.0)
        if tc > 0:
            h = h + jnp.where(col == 0, v_ref[tc - 1, GUARD + TILE - 1 : GUARD + TILE - 1 + CELLS, :], 0.0)
        if tc < TCOLS - 1:
            h = h + jnp.where(
                col == TILE - 1, v_ref[tc + 1, GUARD - TILE + 1 : GUARD - TILE + 1 + CELLS, :], 0.0
            )
        o_ref[tc] = h / 9.0


def box_average(w, up, down):
    slots, cells, emb = w.shape
    rows = slots // TCOLS
    col = jnp.broadcast_to((jnp.arange(cells, dtype=jnp.int32) % TILE)[:, None], (cells, emb))
    return pl.pallas_call(
        box_kernel,
        grid=(rows,),
        in_specs=[
            pl.BlockSpec((slots, cells, emb), lambda r: (0, 0, 0)),
            pl.BlockSpec((TCOLS, TILE, emb), lambda r: (0, 0, 0)),
            pl.BlockSpec((TCOLS, TILE, emb), lambda r: (0, 0, 0)),
            pl.BlockSpec((cells, emb), lambda r: (0, 0)),
        ],
        out_specs=pl.BlockSpec((TCOLS, cells, emb), lambda r: (r, 0, 0)),
        out_shape=jax.ShapeDtypeStruct(w.shape, jnp.float32),
        scratch_shapes=[
            pltpu.VMEM((2 * TILE + CELLS, emb), jnp.float32),
            pltpu.VMEM((TCOLS, 2 * GUARD + CELLS, emb), jnp.float32),
        ],
        compiler_params=pltpu.CompilerParams(
            dimension_semantics=("arbitrary",), vmem_limit_bytes=48 * 1024 * 1024
        ),
        cost_estimate=pl.CostEstimate(
            flops=10 * slots * cells * emb, transcendentals=0, bytes_accessed=8 * slots * cells * emb
        ),
    )(w, up, down, col)


def per_device(
    tiles, counts, tissue_mask, w_reduce, b_reduce, w_spatial, b_spatial, w_expand, proj_w
):
    slots = tiles.shape[2]
    held = counts[0]
    positions = jnp.arange(slots, dtype=jnp.int32)
    alive = positions < held[0]
    weight = jnp.where(alive[:, None], tissue_mask[0, 0], 0).astype(jnp.float32)
    weighted = tile_features(
        held, tiles[0, 0], weight[:, :, None], w_reduce, b_reduce, w_spatial, b_spatial, w_expand, proj_w
    )
    count = lax.axis_size("region")
    forward = [(i, i + 1) for i in range(count - 1)]
    backward = [(target, source) for source, target in forward]
    up = lax.ppermute(weighted[slots - TCOLS :, CELLS - TILE :], "region", forward)
    down = lax.ppermute(weighted[:TCOLS, :TILE], "region", backward)
    averaged = box_average(weighted, up, down)
    return averaged.reshape(1, 1, slots, CELLS, -1)


def solution(mesh):
    placed = (
        P("slide", "region", None, None, None),
        P("slide", "region"),
        P("slide", "region", None, None),
        P(),
        P(),
        P(),
        P(),
        P(),
        P(),
    )
    return jax.shard_map(
        per_device,
        mesh=mesh,
        in_specs=placed,
        out_specs=P("slide", "region", None, None, None),
        check_vma=False,
    )
```

```python
import jax
import jax.numpy as jnp
from jax import lax
from jax.experimental import pallas as pl
from jax.experimental.pallas import tpu as pltpu
from jax.sharding import PartitionSpec as P

CHAN = 1024
MID = 256
TILE = 14
BLOCKS = 2
TCOLS = 4
CELLS = TILE * TILE
WIDE = 16
PADDED = TILE * WIDE


GROUP = 16
SPAN = 2 * TILE
ROWS = SPAN * GROUP
EDGE = TILE * GROUP


def cell_kernel(
    count_ref, x_ref, m_ref, wr_ref, br_ref, ws_ref, bs_ref, we_ref, pw_ref, o_ref,
    cur_ref, r_ref, c_ref,
):
    g = pl.program_id(0)
    total = CELLS * GROUP
    chunks = CELLS // SPAN

    @pl.when(g * GROUP >= count_ref[0])
    def _():
        o_ref[...] = jnp.zeros(o_ref.shape, o_ref.dtype)

    @pl.when(g * GROUP < count_ref[0])
    def _():
        r_ref[0:GROUP, :] = jnp.zeros((GROUP, MID), jnp.float32)
        r_ref[GROUP + total :, :] = jnp.zeros((GROUP, MID), jnp.float32)
        c_ref[0:EDGE, :] = jnp.zeros((EDGE, 3 * MID), jnp.bfloat16)
        c_ref[EDGE + total :, :] = jnp.zeros((EDGE, 3 * MID), jnp.bfloat16)
        lane = lax.broadcasted_iota(jnp.int32, (SPAN, GROUP, MID), 0)
        keep_left = (lane != 0) & (lane != TILE)
        keep_right = (lane != TILE - 1) & (lane != SPAN - 1)

        def source(b, q0):
            if b == 0:
                return x_ref[pl.ds(q0 // GROUP, SPAN)].reshape(ROWS, CHAN)
            return cur_ref[pl.ds(q0, ROWS), :]

        for b in range(BLOCKS):
            for ch in range(chunks):
                q0 = ch * ROWS
                r = jnp.dot(source(b, q0), wr_ref[b], preferred_element_type=jnp.float32)
                r_ref[pl.ds(GROUP + q0, ROWS), :] = jnp.maximum(r + br_ref[b], 0.0)
            for ch in range(chunks):
                q0 = ch * ROWS
                left = r_ref[pl.ds(q0, ROWS), :].reshape(SPAN, GROUP, MID)
                centre = r_ref[pl.ds(GROUP + q0, ROWS), :]
                right = r_ref[pl.ds(2 * GROUP + q0, ROWS), :].reshape(SPAN, GROUP, MID)
                left = jnp.where(keep_left, left, 0.0).reshape(ROWS, MID)
                right = jnp.where(keep_right, right, 0.0).reshape(ROWS, MID)
                c_ref[pl.ds(EDGE + q0, ROWS), 0:MID] = left.astype(jnp.bfloat16)
                c_ref[pl.ds(EDGE + q0, ROWS), MID : 2 * MID] = centre.astype(jnp.bfloat16)
                c_ref[pl.ds(EDGE + q0, ROWS), 2 * MID :] = right.astype(jnp.bfloat16)
            for ch in range(chunks):
                q0 = ch * ROWS
                acc = jnp.dot(c_ref[pl.ds(q0, ROWS), :], ws_ref[b, 0], preferred_element_type=jnp.float32)
                acc += jnp.dot(c_ref[pl.ds(EDGE + q0, ROWS), :], ws_ref[b, 1], preferred_element_type=jnp.float32)
                acc += jnp.dot(c_ref[pl.ds(2 * EDGE + q0, ROWS), :], ws_ref[b, 2], preferred_element_type=jnp.float32)
                spatial = jnp.maximum(acc + bs_ref[b], 0.0).astype(jnp.bfloat16)
                e = jnp.dot(spatial, we_ref[b], preferred_element_type=jnp.float32)
                res = source(b, q0).astype(jnp.float32)
                cur_ref[pl.ds(q0, ROWS), :] = jnp.maximum(res + e, 0.0).astype(jnp.bfloat16)
        for ch in range(chunks):
            q0 = ch * ROWS
            proj = jnp.dot(cur_ref[pl.ds(q0, ROWS), :], pw_ref[...], preferred_element_type=jnp.float32)
            c0 = ch * SPAN
            o_ref[pl.ds(c0, SPAN)] = proj.reshape(SPAN, GROUP, -1) * m_ref[pl.ds(c0, SPAN)]


def cell_features(count, xt, weight, w_reduce, b_reduce, w_spatial, b_spatial, w_expand, proj_w):
    cells, slots, _ = xt.shape
    emb = proj_w.shape[1]
    ws = w_spatial.reshape(BLOCKS, 3, 3 * MID, MID)
    br = b_reduce.reshape(BLOCKS, 1, MID)
    bs = b_spatial.reshape(BLOCKS, 1, MID)

    def live(g, c):
        return (0, jnp.maximum(jnp.minimum(g, (c[0] - 1) // GROUP), 0), 0)

    def whole(nd):
        return lambda g, c: (0,) * nd

    once = pl.Buffered(1)
    grid_spec = pltpu.PrefetchScalarGridSpec(
        num_scalar_prefetch=1,
        grid=(slots // GROUP,),
        in_specs=[
            pl.BlockSpec((cells, GROUP, CHAN), live),
            pl.BlockSpec((cells, GROUP, 1), lambda g, c: (0, g, 0)),
            pl.BlockSpec((BLOCKS, CHAN, MID), whole(3), pipeline_mode=once),
            pl.BlockSpec((BLOCKS, 1, MID), whole(3), pipeline_mode=once),
            pl.BlockSpec((BLOCKS, 3, 3 * MID, MID), whole(4), pipeline_mode=once),
            pl.BlockSpec((BLOCKS, 1, MID), whole(3), pipeline_mode=once),
            pl.BlockSpec((BLOCKS, MID, CHAN), whole(3), pipeline_mode=once),
            pl.BlockSpec((CHAN, emb), whole(2), pipeline_mode=once),
        ],
        out_specs=pl.BlockSpec((cells, GROUP, emb), lambda g, c: (0, g, 0)),
        scratch_shapes=[
            pltpu.VMEM((cells * GROUP, CHAN), jnp.bfloat16),
            pltpu.VMEM((cells * GROUP + 2 * GROUP, MID), jnp.float32),
            pltpu.VMEM((cells * GROUP + 2 * EDGE, 3 * MID), jnp.bfloat16),
        ],
    )
    flops = 2 * slots * cells * (BLOCKS * (2 * CHAN * MID + 9 * MID * MID) + CHAN * emb)
    return pl.pallas_call(
        cell_kernel,
        grid_spec=grid_spec,
        out_shape=jax.ShapeDtypeStruct((cells, slots, emb), jnp.float32),
        compiler_params=pltpu.CompilerParams(
            dimension_semantics=("arbitrary",), vmem_limit_bytes=60 * 1024 * 1024
        ),
        cost_estimate=pl.CostEstimate(
            flops=flops, transcendentals=0, bytes_accessed=slots * cells * (2 * CHAN + 4 * emb + 4)
        ),
    )(count, xt, weight, w_reduce, br, ws, bs, w_expand, proj_w)


GUARD = 16


def box_kernel(w_ref, hu_ref, hd_ref, j_ref, o_ref, g_ref, v_ref):
    tr = pl.program_id(0)
    rows = pl.num_programs(0)
    col = j_ref[...]
    for tc in range(TCOLS):
        t = tr * TCOLS + tc
        g_ref[TILE : TILE + CELLS, :] = w_ref[t]

        @pl.when(tr == 0)
        def _():
            g_ref[0:TILE, :] = hu_ref[tc]

        @pl.when(tr > 0)
        def _():
            g_ref[0:TILE, :] = w_ref[t - TCOLS, CELLS - TILE : CELLS, :]

        @pl.when(tr == rows - 1)
        def _():
            g_ref[TILE + CELLS : 2 * TILE + CELLS, :] = hd_ref[tc]

        @pl.when(tr < rows - 1)
        def _():
            g_ref[TILE + CELLS : 2 * TILE + CELLS, :] = w_ref[t + TCOLS, 0:TILE, :]

        v = g_ref[0:CELLS, :] + g_ref[TILE : TILE + CELLS, :] + g_ref[2 * TILE : 2 * TILE + CELLS, :]
        v_ref[tc, GUARD : GUARD + CELLS, :] = v
    for tc in range(TCOLS):
        h = v_ref[tc, GUARD : GUARD + CELLS, :]
        h = h + jnp.where(col != 0, v_ref[tc, GUARD - 1 : GUARD - 1 + CELLS, :], 0.0)
        h = h + jnp.where(col != TILE - 1, v_ref[tc, GUARD + 1 : GUARD + 1 + CELLS, :], 0.0)
        if tc > 0:
            h = h + jnp.where(col == 0, v_ref[tc - 1, GUARD + TILE - 1 : GUARD + TILE - 1 + CELLS, :], 0.0)
        if tc < TCOLS - 1:
            h = h + jnp.where(
                col == TILE - 1, v_ref[tc + 1, GUARD - TILE + 1 : GUARD - TILE + 1 + CELLS, :], 0.0
            )
        o_ref[tc] = h / 9.0


def box_average(w, up, down):
    slots, cells, emb = w.shape
    rows = slots // TCOLS
    col = jnp.broadcast_to((jnp.arange(cells, dtype=jnp.int32) % TILE)[:, None], (cells, emb))
    return pl.pallas_call(
        box_kernel,
        grid=(rows,),
        in_specs=[
            pl.BlockSpec((slots, cells, emb), lambda r: (0, 0, 0)),
            pl.BlockSpec((TCOLS, TILE, emb), lambda r: (0, 0, 0)),
            pl.BlockSpec((TCOLS, TILE, emb), lambda r: (0, 0, 0)),
            pl.BlockSpec((cells, emb), lambda r: (0, 0)),
        ],
        out_specs=pl.BlockSpec((TCOLS, cells, emb), lambda r: (r, 0, 0)),
        out_shape=jax.ShapeDtypeStruct(w.shape, jnp.float32),
        scratch_shapes=[
            pltpu.VMEM((2 * TILE + CELLS, emb), jnp.float32),
            pltpu.VMEM((TCOLS, 2 * GUARD + CELLS, emb), jnp.float32),
        ],
        compiler_params=pltpu.CompilerParams(
            dimension_semantics=("arbitrary",), vmem_limit_bytes=48 * 1024 * 1024
        ),
        cost_estimate=pl.CostEstimate(
            flops=10 * slots * cells * emb, transcendentals=0, bytes_accessed=8 * slots * cells * emb
        ),
    )(w, up, down, col)


def per_device(
    tiles, counts, tissue_mask, w_reduce, b_reduce, w_spatial, b_spatial, w_expand, proj_w
):
    slots = tiles.shape[2]
    held = counts[0]
    positions = jnp.arange(slots, dtype=jnp.int32)
    alive = positions < held[0]
    weight = jnp.where(alive[:, None], tissue_mask[0, 0], 0).astype(jnp.float32)
    computed = cell_features(
        held,
        jnp.transpose(tiles[0, 0], (1, 0, 2)),
        weight.T[:, :, None],
        w_reduce,
        b_reduce,
        w_spatial,
        b_spatial,
        w_expand,
        proj_w,
    )
    weighted = jnp.transpose(computed, (1, 0, 2))
    count = lax.axis_size("region")
    forward = [(i, i + 1) for i in range(count - 1)]
    backward = [(target, source) for source, target in forward]
    up = lax.ppermute(weighted[slots - TCOLS :, CELLS - TILE :], "region", forward)
    down = lax.ppermute(weighted[:TCOLS, :TILE], "region", backward)
    averaged = box_average(weighted, up, down)
    return averaged.reshape(1, 1, slots, CELLS, -1)


def solution(mesh):
    placed = (
        P("slide", "region", None, None, None),
        P("slide", "region"),
        P("slide", "region", None, None),
        P(),
        P(),
        P(),
        P(),
        P(),
        P(),
    )
    return jax.shard_map(
        per_device,
        mesh=mesh,
        in_specs=placed,
        out_specs=P("slide", "region", None, None, None),
        check_vma=False,
    )
```

```python
import jax
import jax.numpy as jnp
from jax import lax
from jax.experimental import pallas as pl
from jax.experimental.pallas import tpu as pltpu
from jax.sharding import PartitionSpec as P

CHAN = 1024
MID = 256
TILE = 14
BLOCKS = 2
TCOLS = 4
CELLS = TILE * TILE
WIDE = 16
PADDED = TILE * WIDE


GROUP = 16
SPAN = 2 * TILE
ROWS = SPAN * GROUP
EDGE = TILE * GROUP


def cell_kernel(
    count_ref, x_ref, m_ref, wr_ref, br_ref, ws_ref, bs_ref, we_ref, pw_ref, o_ref,
    cur_ref, r_ref, c_ref,
):
    g = pl.program_id(0)
    total = CELLS * GROUP
    chunks = CELLS // SPAN

    @pl.when(g * GROUP >= count_ref[0])
    def _():
        o_ref[...] = jnp.zeros(o_ref.shape, o_ref.dtype)

    @pl.when(g * GROUP < count_ref[0])
    def _():
        r_ref[0:GROUP, :] = jnp.zeros((GROUP, MID), jnp.float32)
        r_ref[GROUP + total :, :] = jnp.zeros((GROUP, MID), jnp.float32)
        c_ref[0:EDGE, :] = jnp.zeros((EDGE, 3 * MID), jnp.bfloat16)
        c_ref[EDGE + total :, :] = jnp.zeros((EDGE, 3 * MID), jnp.bfloat16)
        lane = lax.broadcasted_iota(jnp.int32, (SPAN, GROUP, MID), 0)
        keep_left = (lane != 0) & (lane != TILE)
        keep_right = (lane != TILE - 1) & (lane != SPAN - 1)

        def source(b, q0):
            if b == 0:
                return x_ref[pl.ds(q0 // GROUP, SPAN)].reshape(ROWS, CHAN)
            return cur_ref[pl.ds(q0, ROWS), :]

        for b in range(BLOCKS):
            for ch in range(chunks):
                q0 = ch * ROWS
                r = jnp.dot(source(b, q0), wr_ref[b], preferred_element_type=jnp.float32)
                r_ref[pl.ds(GROUP + q0, ROWS), :] = jnp.maximum(r + br_ref[b], 0.0)
            for ch in range(chunks):
                q0 = ch * ROWS
                left = r_ref[pl.ds(q0, ROWS), :].reshape(SPAN, GROUP, MID)
                centre = r_ref[pl.ds(GROUP + q0, ROWS), :]
                right = r_ref[pl.ds(2 * GROUP + q0, ROWS), :].reshape(SPAN, GROUP, MID)
                left = jnp.where(keep_left, left, 0.0).reshape(ROWS, MID)
                right = jnp.where(keep_right, right, 0.0).reshape(ROWS, MID)
                c_ref[pl.ds(EDGE + q0, ROWS), 0:MID] = left.astype(jnp.bfloat16)
                c_ref[pl.ds(EDGE + q0, ROWS), MID : 2 * MID] = centre.astype(jnp.bfloat16)
                c_ref[pl.ds(EDGE + q0, ROWS), 2 * MID :] = right.astype(jnp.bfloat16)
            for ch in range(chunks):
                q0 = ch * ROWS
                acc = jnp.dot(c_ref[pl.ds(q0, ROWS), :], ws_ref[b, 0], preferred_element_type=jnp.float32)
                acc += jnp.dot(c_ref[pl.ds(EDGE + q0, ROWS), :], ws_ref[b, 1], preferred_element_type=jnp.float32)
                acc += jnp.dot(c_ref[pl.ds(2 * EDGE + q0, ROWS), :], ws_ref[b, 2], preferred_element_type=jnp.float32)
                spatial = jnp.maximum(acc + bs_ref[b], 0.0).astype(jnp.bfloat16)
                e = jnp.dot(spatial, we_ref[b], preferred_element_type=jnp.float32)
                res = source(b, q0).astype(jnp.float32)
                cur_ref[pl.ds(q0, ROWS), :] = jnp.maximum(res + e, 0.0).astype(jnp.bfloat16)
        for ch in range(chunks):
            q0 = ch * ROWS
            proj = jnp.dot(cur_ref[pl.ds(q0, ROWS), :], pw_ref[...], preferred_element_type=jnp.float32)
            c0 = ch * SPAN
            o_ref[pl.ds(c0, SPAN)] = proj.reshape(SPAN, GROUP, -1) * m_ref[pl.ds(c0, SPAN)]


def cell_features(count, xt, weight, w_reduce, b_reduce, w_spatial, b_spatial, w_expand, proj_w):
    cells, slots, _ = xt.shape
    emb = proj_w.shape[1]
    ws = w_spatial.reshape(BLOCKS, 3, 3 * MID, MID)
    br = b_reduce.reshape(BLOCKS, 1, MID)
    bs = b_spatial.reshape(BLOCKS, 1, MID)

    def live(g, c):
        return (0, jnp.maximum(jnp.minimum(g, (c[0] - 1) // GROUP), 0), 0)

    def whole(nd):
        return lambda g, c: (0,) * nd

    once = pl.Buffered(1)
    grid_spec = pltpu.PrefetchScalarGridSpec(
        num_scalar_prefetch=1,
        grid=(slots // GROUP,),
        in_specs=[
            pl.BlockSpec((cells, GROUP, CHAN), live),
            pl.BlockSpec((cells, GROUP, 1), lambda g, c: (0, g, 0)),
            pl.BlockSpec((BLOCKS, CHAN, MID), whole(3), pipeline_mode=once),
            pl.BlockSpec((BLOCKS, 1, MID), whole(3), pipeline_mode=once),
            pl.BlockSpec((BLOCKS, 3, 3 * MID, MID), whole(4), pipeline_mode=once),
            pl.BlockSpec((BLOCKS, 1, MID), whole(3), pipeline_mode=once),
            pl.BlockSpec((BLOCKS, MID, CHAN), whole(3), pipeline_mode=once),
            pl.BlockSpec((CHAN, emb), whole(2), pipeline_mode=once),
        ],
        out_specs=pl.BlockSpec((cells, GROUP, emb), lambda g, c: (0, g, 0)),
        scratch_shapes=[
            pltpu.VMEM((cells * GROUP, CHAN), jnp.bfloat16),
            pltpu.VMEM((cells * GROUP + 2 * GROUP, MID), jnp.float32),
            pltpu.VMEM((cells * GROUP + 2 * EDGE, 3 * MID), jnp.bfloat16),
        ],
    )
    flops = 2 * slots * cells * (BLOCKS * (2 * CHAN * MID + 9 * MID * MID) + CHAN * emb)
    return pl.pallas_call(
        cell_kernel,
        grid_spec=grid_spec,
        out_shape=jax.ShapeDtypeStruct((cells, slots, emb), jnp.float32),
        compiler_params=pltpu.CompilerParams(
            dimension_semantics=("arbitrary",), vmem_limit_bytes=60 * 1024 * 1024
        ),
        cost_estimate=pl.CostEstimate(
            flops=flops, transcendentals=0, bytes_accessed=slots * cells * (2 * CHAN + 4 * emb + 4)
        ),
    )(count, xt, weight, w_reduce, br, ws, bs, w_expand, proj_w)


def grid_box_kernel(w_ref, hu_ref, hd_ref, o_ref, v_ref, ub_ref, db_ref, sh_ref):
    slots = w_ref.shape[2]
    ub_ref[:, 8 : 8 + slots, :] = w_ref[TILE - 1]
    ub_ref[:, 4:8, :] = hu_ref[...]
    db_ref[:, 0:slots, :] = w_ref[0]
    db_ref[:, slots : slots + 4, :] = hd_ref[...]
    v_ref[0] = ub_ref[:, 4 : 4 + slots, :] + w_ref[0] + w_ref[1]
    v_ref[TILE - 1] = w_ref[TILE - 2] + w_ref[TILE - 1] + db_ref[:, 4 : 4 + slots, :]

    def vertical(i, carry):
        v_ref[i] = w_ref[i - 1] + w_ref[i] + w_ref[i + 1]
        return carry

    lax.fori_loop(1, TILE - 1, vertical, 0)
    slot = lax.broadcasted_iota(jnp.int32, (slots, w_ref.shape[3]), 0) & (TCOLS - 1)

    def horizontal(i, carry):
        o_ref[i, 1 : TILE - 1] = (
            v_ref[i, 0 : TILE - 2] + v_ref[i, 1 : TILE - 1] + v_ref[i, 2:TILE]
        ) / 9.0
        sh_ref[8 : 8 + slots, :] = v_ref[i, TILE - 1]
        left = jnp.where(slot != 0, sh_ref[7 : 7 + slots, :], 0.0)
        o_ref[i, 0] = (left + v_ref[i, 0] + v_ref[i, 1]) / 9.0
        sh_ref[8 : 8 + slots, :] = v_ref[i, 0]
        right = jnp.where(slot != TCOLS - 1, sh_ref[9 : 9 + slots, :], 0.0)
        o_ref[i, TILE - 1] = (v_ref[i, TILE - 2] + v_ref[i, TILE - 1] + right) / 9.0
        return carry

    lax.fori_loop(0, TILE, horizontal, 0)


def grid_box_average(w, up, down):
    cells, slots, emb = w.shape
    w4 = w.reshape(TILE, TILE, slots, emb)
    out = pl.pallas_call(
        grid_box_kernel,
        out_shape=jax.ShapeDtypeStruct(w4.shape, jnp.float32),
        scratch_shapes=[
            pltpu.VMEM(w4.shape, jnp.float32),
            pltpu.VMEM((TILE, slots + 8, emb), jnp.float32),
            pltpu.VMEM((TILE, slots + 8, emb), jnp.float32),
            pltpu.VMEM((slots + 16, emb), jnp.float32),
        ],
        compiler_params=pltpu.CompilerParams(vmem_limit_bytes=48 * 1024 * 1024),
        cost_estimate=pl.CostEstimate(
            flops=10 * slots * cells * emb, transcendentals=0, bytes_accessed=8 * slots * cells * emb
        ),
    )(w4, up, down)
    return out.reshape(cells, slots, emb)


def per_device(
    tiles, counts, tissue_mask, w_reduce, b_reduce, w_spatial, b_spatial, w_expand, proj_w
):
    slots = tiles.shape[2]
    held = counts[0]
    positions = jnp.arange(slots, dtype=jnp.int32)
    alive = positions < held[0]
    weight = jnp.where(alive[:, None], tissue_mask[0, 0], 0).astype(jnp.float32)
    computed = cell_features(
        held,
        jnp.transpose(tiles[0, 0], (1, 0, 2)),
        weight.T[:, :, None],
        w_reduce,
        b_reduce,
        w_spatial,
        b_spatial,
        w_expand,
        proj_w,
    )
    count = lax.axis_size("region")
    forward = [(i, i + 1) for i in range(count - 1)]
    backward = [(target, source) for source, target in forward]
    up = lax.ppermute(computed[CELLS - TILE :, slots - TCOLS :], "region", forward)
    down = lax.ppermute(computed[:TILE, :TCOLS], "region", backward)
    averaged = grid_box_average(computed, up, down)
    return jnp.transpose(averaged, (1, 0, 2)).reshape(1, 1, slots, CELLS, -1)


def solution(mesh):
    placed = (
        P("slide", "region", None, None, None),
        P("slide", "region"),
        P("slide", "region", None, None),
        P(),
        P(),
        P(),
        P(),
        P(),
        P(),
    )
    return jax.shard_map(
        per_device,
        mesh=mesh,
        in_specs=placed,
        out_specs=P("slide", "region", None, None, None),
        check_vma=False,
    )
```

```python
import jax
import jax.numpy as jnp
from jax import lax
from jax.experimental import pallas as pl
from jax.experimental.pallas import tpu as pltpu
from jax.sharding import PartitionSpec as P

CHAN = 1024
MID = 256
TILE = 14
BLOCKS = 2
TCOLS = 4
CELLS = TILE * TILE
WIDE = 16
PADDED = TILE * WIDE


GROUP = 16
SPAN = 7 * TILE
ROWS = SPAN * GROUP
EDGE = TILE * GROUP


def cell_kernel(
    count_ref, x_ref, m_ref, wr_ref, br_ref, ws_ref, bs_ref, we_ref, pw_ref, o_ref,
    cur_ref, r_ref, c_ref,
):
    g = pl.program_id(0)
    total = CELLS * GROUP
    chunks = CELLS // SPAN

    @pl.when(g * GROUP >= count_ref[0])
    def _():
        o_ref[...] = jnp.zeros(o_ref.shape, o_ref.dtype)

    @pl.when(g * GROUP < count_ref[0])
    def _():
        r_ref[0:GROUP, :] = jnp.zeros((GROUP, MID), jnp.float32)
        r_ref[GROUP + total :, :] = jnp.zeros((GROUP, MID), jnp.float32)
        c_ref[0:EDGE, :] = jnp.zeros((EDGE, 3 * MID), jnp.bfloat16)
        c_ref[EDGE + total :, :] = jnp.zeros((EDGE, 3 * MID), jnp.bfloat16)
        lane = lax.broadcasted_iota(jnp.int32, (SPAN, GROUP, MID), 0)
        keep_left = lane != 0
        keep_right = lane != TILE - 1
        for row in range(1, SPAN // TILE):
            keep_left = keep_left & (lane != TILE * row)
            keep_right = keep_right & (lane != TILE * row + TILE - 1)

        def source(b, q0):
            if b == 0:
                return x_ref[pl.ds(q0 // GROUP, SPAN)].reshape(ROWS, CHAN)
            return cur_ref[pl.ds(q0, ROWS), :]

        for b in range(BLOCKS):
            for ch in range(chunks):
                q0 = ch * ROWS
                r = jnp.dot(source(b, q0), wr_ref[b], preferred_element_type=jnp.float32)
                r_ref[pl.ds(GROUP + q0, ROWS), :] = jnp.maximum(r + br_ref[b], 0.0)
            for ch in range(chunks):
                q0 = ch * ROWS
                left = r_ref[pl.ds(q0, ROWS), :].reshape(SPAN, GROUP, MID)
                centre = r_ref[pl.ds(GROUP + q0, ROWS), :]
                right = r_ref[pl.ds(2 * GROUP + q0, ROWS), :].reshape(SPAN, GROUP, MID)
                left = jnp.where(keep_left, left, 0.0).reshape(ROWS, MID)
                right = jnp.where(keep_right, right, 0.0).reshape(ROWS, MID)
                c_ref[pl.ds(EDGE + q0, ROWS), 0:MID] = left.astype(jnp.bfloat16)
                c_ref[pl.ds(EDGE + q0, ROWS), MID : 2 * MID] = centre.astype(jnp.bfloat16)
                c_ref[pl.ds(EDGE + q0, ROWS), 2 * MID :] = right.astype(jnp.bfloat16)
            for ch in range(chunks):
                q0 = ch * ROWS
                acc = jnp.dot(c_ref[pl.ds(q0, ROWS), :], ws_ref[b, 0], preferred_element_type=jnp.float32)
                acc += jnp.dot(c_ref[pl.ds(EDGE + q0, ROWS), :], ws_ref[b, 1], preferred_element_type=jnp.float32)
                acc += jnp.dot(c_ref[pl.ds(2 * EDGE + q0, ROWS), :], ws_ref[b, 2], preferred_element_type=jnp.float32)
                spatial = jnp.maximum(acc + bs_ref[b], 0.0).astype(jnp.bfloat16)
                e = jnp.dot(spatial, we_ref[b], preferred_element_type=jnp.float32)
                res = source(b, q0).astype(jnp.float32)
                cur_ref[pl.ds(q0, ROWS), :] = jnp.maximum(res + e, 0.0).astype(jnp.bfloat16)
        for ch in range(chunks):
            q0 = ch * ROWS
            proj = jnp.dot(cur_ref[pl.ds(q0, ROWS), :], pw_ref[...], preferred_element_type=jnp.float32)
            c0 = ch * SPAN
            o_ref[pl.ds(c0, SPAN)] = proj.reshape(SPAN, GROUP, -1) * m_ref[pl.ds(c0, SPAN)]


def cell_features(count, xt, weight, w_reduce, b_reduce, w_spatial, b_spatial, w_expand, proj_w):
    cells, slots, _ = xt.shape
    emb = proj_w.shape[1]
    ws = w_spatial.reshape(BLOCKS, 3, 3 * MID, MID)
    br = b_reduce.reshape(BLOCKS, 1, MID)
    bs = b_spatial.reshape(BLOCKS, 1, MID)

    def live(g, c):
        return (0, jnp.maximum(jnp.minimum(g, (c[0] - 1) // GROUP), 0), 0)

    def whole(nd):
        return lambda g, c: (0,) * nd

    once = pl.Buffered(1)
    grid_spec = pltpu.PrefetchScalarGridSpec(
        num_scalar_prefetch=1,
        grid=(slots // GROUP,),
        in_specs=[
            pl.BlockSpec((cells, GROUP, CHAN), live),
            pl.BlockSpec((cells, GROUP, 1), lambda g, c: (0, g, 0)),
            pl.BlockSpec((BLOCKS, CHAN, MID), whole(3), pipeline_mode=once),
            pl.BlockSpec((BLOCKS, 1, MID), whole(3), pipeline_mode=once),
            pl.BlockSpec((BLOCKS, 3, 3 * MID, MID), whole(4), pipeline_mode=once),
            pl.BlockSpec((BLOCKS, 1, MID), whole(3), pipeline_mode=once),
            pl.BlockSpec((BLOCKS, MID, CHAN), whole(3), pipeline_mode=once),
            pl.BlockSpec((CHAN, emb), whole(2), pipeline_mode=once),
        ],
        out_specs=pl.BlockSpec((cells, GROUP, emb), lambda g, c: (0, g, 0)),
        scratch_shapes=[
            pltpu.VMEM((cells * GROUP, CHAN), jnp.bfloat16),
            pltpu.VMEM((cells * GROUP + 2 * GROUP, MID), jnp.float32),
            pltpu.VMEM((cells * GROUP + 2 * EDGE, 3 * MID), jnp.bfloat16),
        ],
    )
    flops = 2 * slots * cells * (BLOCKS * (2 * CHAN * MID + 9 * MID * MID) + CHAN * emb)
    return pl.pallas_call(
        cell_kernel,
        grid_spec=grid_spec,
        out_shape=jax.ShapeDtypeStruct((cells, slots, emb), jnp.float32),
        compiler_params=pltpu.CompilerParams(
            dimension_semantics=("arbitrary",), vmem_limit_bytes=60 * 1024 * 1024
        ),
        cost_estimate=pl.CostEstimate(
            flops=flops, transcendentals=0, bytes_accessed=slots * cells * (2 * CHAN + 4 * emb + 4)
        ),
    )(count, xt, weight, w_reduce, br, ws, bs, w_expand, proj_w)


def grid_box_kernel(w_ref, hu_ref, hd_ref, o_ref, v_ref, ub_ref, db_ref, sh_ref):
    slots = w_ref.shape[2]
    ub_ref[:, 8 : 8 + slots, :] = w_ref[TILE - 1]
    ub_ref[:, 4:8, :] = hu_ref[...]
    db_ref[:, 0:slots, :] = w_ref[0]
    db_ref[:, slots : slots + 4, :] = hd_ref[...]
    v_ref[0] = ub_ref[:, 4 : 4 + slots, :] + w_ref[0] + w_ref[1]
    v_ref[TILE - 1] = w_ref[TILE - 2] + w_ref[TILE - 1] + db_ref[:, 4 : 4 + slots, :]

    def vertical(i, carry):
        v_ref[i] = w_ref[i - 1] + w_ref[i] + w_ref[i + 1]
        return carry

    lax.fori_loop(1, TILE - 1, vertical, 0)
    slot = lax.broadcasted_iota(jnp.int32, (slots, w_ref.shape[3]), 0) & (TCOLS - 1)

    def horizontal(i, carry):
        o_ref[i, 1 : TILE - 1] = (
            v_ref[i, 0 : TILE - 2] + v_ref[i, 1 : TILE - 1] + v_ref[i, 2:TILE]
        ) / 9.0
        sh_ref[8 : 8 + slots, :] = v_ref[i, TILE - 1]
        left = jnp.where(slot != 0, sh_ref[7 : 7 + slots, :], 0.0)
        o_ref[i, 0] = (left + v_ref[i, 0] + v_ref[i, 1]) / 9.0
        sh_ref[8 : 8 + slots, :] = v_ref[i, 0]
        right = jnp.where(slot != TCOLS - 1, sh_ref[9 : 9 + slots, :], 0.0)
        o_ref[i, TILE - 1] = (v_ref[i, TILE - 2] + v_ref[i, TILE - 1] + right) / 9.0
        return carry

    lax.fori_loop(0, TILE, horizontal, 0)


def grid_box_average(w, up, down):
    cells, slots, emb = w.shape
    w4 = w.reshape(TILE, TILE, slots, emb)
    out = pl.pallas_call(
        grid_box_kernel,
        out_shape=jax.ShapeDtypeStruct(w4.shape, jnp.float32),
        scratch_shapes=[
            pltpu.VMEM(w4.shape, jnp.float32),
            pltpu.VMEM((TILE, slots + 8, emb), jnp.float32),
            pltpu.VMEM((TILE, slots + 8, emb), jnp.float32),
            pltpu.VMEM((slots + 16, emb), jnp.float32),
        ],
        compiler_params=pltpu.CompilerParams(vmem_limit_bytes=48 * 1024 * 1024),
        cost_estimate=pl.CostEstimate(
            flops=10 * slots * cells * emb, transcendentals=0, bytes_accessed=8 * slots * cells * emb
        ),
    )(w4, up, down)
    return out.reshape(cells, slots, emb)


def per_device(
    tiles, counts, tissue_mask, w_reduce, b_reduce, w_spatial, b_spatial, w_expand, proj_w
):
    slots = tiles.shape[2]
    held = counts[0]
    positions = jnp.arange(slots, dtype=jnp.int32)
    alive = positions < held[0]
    weight = jnp.where(alive[:, None], tissue_mask[0, 0], 0).astype(jnp.float32)
    computed = cell_features(
        held,
        jnp.transpose(tiles[0, 0], (1, 0, 2)),
        weight.T[:, :, None],
        w_reduce,
        b_reduce,
        w_spatial,
        b_spatial,
        w_expand,
        proj_w,
    )
    count = lax.axis_size("region")
    forward = [(i, i + 1) for i in range(count - 1)]
    backward = [(target, source) for source, target in forward]
    up = lax.ppermute(computed[CELLS - TILE :, slots - TCOLS :], "region", forward)
    down = lax.ppermute(computed[:TILE, :TCOLS], "region", backward)
    averaged = grid_box_average(computed, up, down)
    return jnp.transpose(averaged, (1, 0, 2)).reshape(1, 1, slots, CELLS, -1)


def solution(mesh):
    placed = (
        P("slide", "region", None, None, None),
        P("slide", "region"),
        P("slide", "region", None, None),
        P(),
        P(),
        P(),
        P(),
        P(),
        P(),
    )
    return jax.shard_map(
        per_device,
        mesh=mesh,
        in_specs=placed,
        out_specs=P("slide", "region", None, None, None),
        check_vma=False,
    )
```

```python
import jax
import jax.numpy as jnp
from jax import lax
from jax.experimental import pallas as pl
from jax.experimental.pallas import tpu as pltpu
from jax.sharding import PartitionSpec as P

CHAN = 1024
MID = 256
TILE = 14
BLOCKS = 2
TCOLS = 4
CELLS = TILE * TILE
WIDE = 16
PADDED = TILE * WIDE


GROUP = 16
SPAN = 7 * TILE
ROWS = SPAN * GROUP
EDGE = TILE * GROUP


def cell_kernel(
    count_ref, x_ref, m_ref, wr_ref, br_ref, ws_ref, bs_ref, we_ref, pw_ref, o_ref,
    cur_ref, r_ref, c_ref,
):
    g = pl.program_id(0)
    total = CELLS * GROUP
    chunks = CELLS // SPAN

    @pl.when(g * GROUP >= count_ref[0])
    def _():
        o_ref[...] = jnp.zeros(o_ref.shape, o_ref.dtype)

    @pl.when(g * GROUP < count_ref[0])
    def _():
        r_ref[0:GROUP, :] = jnp.zeros((GROUP, MID), jnp.float32)
        r_ref[GROUP + total :, :] = jnp.zeros((GROUP, MID), jnp.float32)
        c_ref[0:EDGE, :] = jnp.zeros((EDGE, 3 * MID), jnp.bfloat16)
        c_ref[EDGE + total :, :] = jnp.zeros((EDGE, 3 * MID), jnp.bfloat16)
        lane = lax.broadcasted_iota(jnp.int32, (SPAN, GROUP, MID), 0)
        keep_left = lane != 0
        keep_right = lane != TILE - 1
        for row in range(1, SPAN // TILE):
            keep_left = keep_left & (lane != TILE * row)
            keep_right = keep_right & (lane != TILE * row + TILE - 1)

        def source(b, q0):
            if b == 0:
                return x_ref[pl.ds(q0 // GROUP, SPAN)].reshape(ROWS, CHAN)
            return cur_ref[pl.ds(q0, ROWS), :]

        for b in range(BLOCKS):
            for ch in range(chunks):
                q0 = ch * ROWS
                r = jnp.dot(source(b, q0), wr_ref[b], preferred_element_type=jnp.float32)
                r_ref[pl.ds(GROUP + q0, ROWS), :] = jnp.maximum(r + br_ref[b : b + 1, :], 0.0)
            for ch in range(chunks):
                q0 = ch * ROWS
                left = r_ref[pl.ds(q0, ROWS), :].reshape(SPAN, GROUP, MID)
                centre = r_ref[pl.ds(GROUP + q0, ROWS), :]
                right = r_ref[pl.ds(2 * GROUP + q0, ROWS), :].reshape(SPAN, GROUP, MID)
                left = jnp.where(keep_left, left, 0.0).reshape(ROWS, MID)
                right = jnp.where(keep_right, right, 0.0).reshape(ROWS, MID)
                c_ref[pl.ds(EDGE + q0, ROWS), 0:MID] = left.astype(jnp.bfloat16)
                c_ref[pl.ds(EDGE + q0, ROWS), MID : 2 * MID] = centre.astype(jnp.bfloat16)
                c_ref[pl.ds(EDGE + q0, ROWS), 2 * MID :] = right.astype(jnp.bfloat16)
            for ch in range(chunks):
                q0 = ch * ROWS
                acc = jnp.dot(c_ref[pl.ds(q0, ROWS), :], ws_ref[b, 0], preferred_element_type=jnp.float32)
                acc += jnp.dot(c_ref[pl.ds(EDGE + q0, ROWS), :], ws_ref[b, 1], preferred_element_type=jnp.float32)
                acc += jnp.dot(c_ref[pl.ds(2 * EDGE + q0, ROWS), :], ws_ref[b, 2], preferred_element_type=jnp.float32)
                spatial = jnp.maximum(acc + bs_ref[b : b + 1, :], 0.0).astype(jnp.bfloat16)
                e = jnp.dot(spatial, we_ref[b], preferred_element_type=jnp.float32)
                res = source(b, q0).astype(jnp.float32)
                cur_ref[pl.ds(q0, ROWS), :] = jnp.maximum(res + e, 0.0).astype(jnp.bfloat16)
        for ch in range(chunks):
            q0 = ch * ROWS
            proj = jnp.dot(cur_ref[pl.ds(q0, ROWS), :], pw_ref[...], preferred_element_type=jnp.float32)
            c0 = ch * SPAN
            o_ref[pl.ds(c0, SPAN)] = proj.reshape(SPAN, GROUP, -1) * m_ref[pl.ds(c0, SPAN)]


def cell_features(count, xt, weight, w_reduce, b_reduce, w_spatial, b_spatial, w_expand, proj_w):
    cells, slots, _ = xt.shape
    emb = proj_w.shape[1]
    ws = w_spatial.reshape(BLOCKS, 3, 3 * MID, MID)
    def live(g, c):
        return (0, jnp.maximum(jnp.minimum(g, (c[0] - 1) // GROUP), 0), 0)

    def whole(nd):
        return lambda g, c: (0,) * nd

    once = pl.Buffered(1)
    grid_spec = pltpu.PrefetchScalarGridSpec(
        num_scalar_prefetch=1,
        grid=(slots // GROUP,),
        in_specs=[
            pl.BlockSpec((cells, GROUP, CHAN), live),
            pl.BlockSpec((cells, GROUP, 1), lambda g, c: (0, g, 0)),
            pl.BlockSpec((BLOCKS, CHAN, MID), whole(3), pipeline_mode=once),
            pl.BlockSpec((BLOCKS, MID), whole(2), pipeline_mode=once),
            pl.BlockSpec((BLOCKS, 3, 3 * MID, MID), whole(4), pipeline_mode=once),
            pl.BlockSpec((BLOCKS, MID), whole(2), pipeline_mode=once),
            pl.BlockSpec((BLOCKS, MID, CHAN), whole(3), pipeline_mode=once),
            pl.BlockSpec((CHAN, emb), whole(2), pipeline_mode=once),
        ],
        out_specs=pl.BlockSpec((cells, GROUP, emb), lambda g, c: (0, g, 0)),
        scratch_shapes=[
            pltpu.VMEM((cells * GROUP, CHAN), jnp.bfloat16),
            pltpu.VMEM((cells * GROUP + 2 * GROUP, MID), jnp.float32),
            pltpu.VMEM((cells * GROUP + 2 * EDGE, 3 * MID), jnp.bfloat16),
        ],
    )
    flops = 2 * slots * cells * (BLOCKS * (2 * CHAN * MID + 9 * MID * MID) + CHAN * emb)
    return pl.pallas_call(
        cell_kernel,
        grid_spec=grid_spec,
        out_shape=jax.ShapeDtypeStruct((cells, slots, emb), jnp.float32),
        compiler_params=pltpu.CompilerParams(
            dimension_semantics=("arbitrary",), vmem_limit_bytes=60 * 1024 * 1024
        ),
        cost_estimate=pl.CostEstimate(
            flops=flops, transcendentals=0, bytes_accessed=slots * cells * (2 * CHAN + 4 * emb + 4)
        ),
    )(count, xt, weight, w_reduce, b_reduce, ws, b_spatial, w_expand, proj_w)


def grid_box_kernel(w_ref, hu_ref, hd_ref, o_ref, v_ref, ub_ref, db_ref, sh_ref):
    slots = w_ref.shape[2]
    ub_ref[:, 8 : 8 + slots, :] = w_ref[TILE - 1]
    ub_ref[:, 4:8, :] = hu_ref[...]
    db_ref[:, 0:slots, :] = w_ref[0]
    db_ref[:, slots : slots + 4, :] = hd_ref[...]
    v_ref[0] = ub_ref[:, 4 : 4 + slots, :] + w_ref[0] + w_ref[1]
    v_ref[TILE - 1] = w_ref[TILE - 2] + w_ref[TILE - 1] + db_ref[:, 4 : 4 + slots, :]

    def vertical(i, carry):
        v_ref[i] = w_ref[i - 1] + w_ref[i] + w_ref[i + 1]
        return carry

    lax.fori_loop(1, TILE - 1, vertical, 0)
    slot = lax.broadcasted_iota(jnp.int32, (slots, w_ref.shape[3]), 0) & (TCOLS - 1)

    def horizontal(i, carry):
        o_ref[i, 1 : TILE - 1] = (
            v_ref[i, 0 : TILE - 2] + v_ref[i, 1 : TILE - 1] + v_ref[i, 2:TILE]
        ) / 9.0
        sh_ref[8 : 8 + slots, :] = v_ref[i, TILE - 1]
        left = jnp.where(slot != 0, sh_ref[7 : 7 + slots, :], 0.0)
        o_ref[i, 0] = (left + v_ref[i, 0] + v_ref[i, 1]) / 9.0
        sh_ref[8 : 8 + slots, :] = v_ref[i, 0]
        right = jnp.where(slot != TCOLS - 1, sh_ref[9 : 9 + slots, :], 0.0)
        o_ref[i, TILE - 1] = (v_ref[i, TILE - 2] + v_ref[i, TILE - 1] + right) / 9.0
        return carry

    lax.fori_loop(0, TILE, horizontal, 0)


def grid_box_average(w, up, down):
    cells, slots, emb = w.shape
    w4 = w.reshape(TILE, TILE, slots, emb)
    out = pl.pallas_call(
        grid_box_kernel,
        out_shape=jax.ShapeDtypeStruct(w4.shape, jnp.float32),
        scratch_shapes=[
            pltpu.VMEM(w4.shape, jnp.float32),
            pltpu.VMEM((TILE, slots + 8, emb), jnp.float32),
            pltpu.VMEM((TILE, slots + 8, emb), jnp.float32),
            pltpu.VMEM((slots + 16, emb), jnp.float32),
        ],
        compiler_params=pltpu.CompilerParams(vmem_limit_bytes=48 * 1024 * 1024),
        cost_estimate=pl.CostEstimate(
            flops=10 * slots * cells * emb, transcendentals=0, bytes_accessed=8 * slots * cells * emb
        ),
    )(w4, up, down)
    return out.reshape(cells, slots, emb)


def per_device(
    tiles, counts, tissue_mask, w_reduce, b_reduce, w_spatial, b_spatial, w_expand, proj_w
):
    slots = tiles.shape[2]
    held = counts[0]
    positions = jnp.arange(slots, dtype=jnp.int32)
    alive = positions < held[0]
    weight = jnp.where(alive[:, None], tissue_mask[0, 0], 0).astype(jnp.float32)
    computed = cell_features(
        held,
        jnp.transpose(tiles[0, 0], (1, 0, 2)),
        weight.T[:, :, None].astype(jnp.bfloat16),
        w_reduce,
        b_reduce,
        w_spatial,
        b_spatial,
        w_expand,
        proj_w,
    )
    count = lax.axis_size("region")
    forward = [(i, i + 1) for i in range(count - 1)]
    backward = [(target, source) for source, target in forward]
    up = lax.ppermute(computed[CELLS - TILE :, slots - TCOLS :], "region", forward)
    down = lax.ppermute(computed[:TILE, :TCOLS], "region", backward)
    averaged = grid_box_average(computed, up, down)
    return jnp.transpose(averaged, (1, 0, 2)).reshape(1, 1, slots, CELLS, -1)


def solution(mesh):
    placed = (
        P("slide", "region", None, None, None),
        P("slide", "region"),
        P("slide", "region", None, None),
        P(),
        P(),
        P(),
        P(),
        P(),
        P(),
    )
    return jax.shard_map(
        per_device,
        mesh=mesh,
        in_specs=placed,
        out_specs=P("slide", "region", None, None, None),
        check_vma=False,
    )
```

```python
import jax
import jax.numpy as jnp
from jax import lax
from jax.experimental import pallas as pl
from jax.experimental.pallas import tpu as pltpu
from jax.sharding import PartitionSpec as P

CHAN = 1024
MID = 256
TILE = 14
BLOCKS = 2
TCOLS = 4
CELLS = TILE * TILE
WIDE = 16
PADDED = TILE * WIDE


GROUP = 16
SPAN = 7 * TILE
ROWS = SPAN * GROUP
EDGE = TILE * GROUP


def cell_kernel(
    count_ref, x_ref, m_ref, wr_ref, br_ref, ws_ref, bs_ref, we_ref, pw_ref, o_ref,
    cur_ref, r_ref, c_ref,
):
    g = pl.program_id(0)
    total = CELLS * GROUP
    chunks = CELLS // SPAN

    @pl.when(g * GROUP >= count_ref[0])
    def _():
        o_ref[...] = jnp.zeros(o_ref.shape, o_ref.dtype)

    @pl.when(g * GROUP < count_ref[0])
    def _():
        r_ref[0:GROUP, :] = jnp.zeros((GROUP, MID), jnp.float32)
        r_ref[GROUP + total :, :] = jnp.zeros((GROUP, MID), jnp.float32)
        c_ref[0:EDGE, :] = jnp.zeros((EDGE, 3 * MID), jnp.bfloat16)
        c_ref[EDGE + total :, :] = jnp.zeros((EDGE, 3 * MID), jnp.bfloat16)
        lane = lax.broadcasted_iota(jnp.int32, (SPAN, GROUP, MID), 0)
        keep_left = lane != 0
        keep_right = lane != TILE - 1
        for row in range(1, SPAN // TILE):
            keep_left = keep_left & (lane != TILE * row)
            keep_right = keep_right & (lane != TILE * row + TILE - 1)

        def source(b, q0):
            if b == 0:
                return x_ref[pl.ds(q0 // GROUP, SPAN)].reshape(ROWS, CHAN)
            return cur_ref[pl.ds(q0, ROWS), :]

        for b in range(BLOCKS):
            for ch in range(chunks):
                q0 = ch * ROWS
                r = jnp.dot(source(b, q0), wr_ref[b], preferred_element_type=jnp.float32)
                r_ref[pl.ds(GROUP + q0, ROWS), :] = jnp.maximum(r + br_ref[b : b + 1, :], 0.0)
            for ch in range(chunks):
                q0 = ch * ROWS
                left = r_ref[pl.ds(q0, ROWS), :].reshape(SPAN, GROUP, MID)
                centre = r_ref[pl.ds(GROUP + q0, ROWS), :]
                right = r_ref[pl.ds(2 * GROUP + q0, ROWS), :].reshape(SPAN, GROUP, MID)
                left = jnp.where(keep_left, left, 0.0).reshape(ROWS, MID)
                right = jnp.where(keep_right, right, 0.0).reshape(ROWS, MID)
                c_ref[pl.ds(EDGE + q0, ROWS), 0:MID] = left.astype(jnp.bfloat16)
                c_ref[pl.ds(EDGE + q0, ROWS), MID : 2 * MID] = centre.astype(jnp.bfloat16)
                c_ref[pl.ds(EDGE + q0, ROWS), 2 * MID :] = right.astype(jnp.bfloat16)
            for ch in range(chunks):
                q0 = ch * ROWS
                acc = jnp.dot(c_ref[pl.ds(q0, ROWS), :], ws_ref[b, 0], preferred_element_type=jnp.float32)
                acc += jnp.dot(c_ref[pl.ds(EDGE + q0, ROWS), :], ws_ref[b, 1], preferred_element_type=jnp.float32)
                acc += jnp.dot(c_ref[pl.ds(2 * EDGE + q0, ROWS), :], ws_ref[b, 2], preferred_element_type=jnp.float32)
                spatial = jnp.maximum(acc + bs_ref[b : b + 1, :], 0.0).astype(jnp.bfloat16)
                e = jnp.dot(spatial, we_ref[b], preferred_element_type=jnp.float32)
                res = source(b, q0).astype(jnp.float32)
                cur_ref[pl.ds(q0, ROWS), :] = jnp.maximum(res + e, 0.0).astype(jnp.bfloat16)
        for ch in range(chunks):
            q0 = ch * ROWS
            proj = jnp.dot(cur_ref[pl.ds(q0, ROWS), :], pw_ref[...], preferred_element_type=jnp.float32)
            c0 = ch * SPAN
            o_ref[pl.ds(c0, SPAN)] = proj.reshape(SPAN, GROUP, -1) * m_ref[pl.ds(c0, SPAN)]


def cell_features(count, xt, weight, w_reduce, b_reduce, w_spatial, b_spatial, w_expand, proj_w):
    cells, slots, _ = xt.shape
    emb = proj_w.shape[1]
    ws = w_spatial.reshape(BLOCKS, 3, 3 * MID, MID)
    def live(g, c):
        return (0, jnp.maximum(jnp.minimum(g, (c[0] - 1) // GROUP), 0), 0)

    def whole(nd):
        return lambda g, c: (0,) * nd

    once = pl.Buffered(1)
    grid_spec = pltpu.PrefetchScalarGridSpec(
        num_scalar_prefetch=1,
        grid=(slots // GROUP,),
        in_specs=[
            pl.BlockSpec((cells, GROUP, CHAN), live),
            pl.BlockSpec((cells, GROUP, 1), lambda g, c: (0, g, 0)),
            pl.BlockSpec((BLOCKS, CHAN, MID), whole(3), pipeline_mode=once),
            pl.BlockSpec((BLOCKS, MID), whole(2), pipeline_mode=once),
            pl.BlockSpec((BLOCKS, 3, 3 * MID, MID), whole(4), pipeline_mode=once),
            pl.BlockSpec((BLOCKS, MID), whole(2), pipeline_mode=once),
            pl.BlockSpec((BLOCKS, MID, CHAN), whole(3), pipeline_mode=once),
            pl.BlockSpec((CHAN, emb), whole(2), pipeline_mode=once),
        ],
        out_specs=pl.BlockSpec((cells, GROUP, emb), lambda g, c: (0, g, 0)),
        scratch_shapes=[
            pltpu.VMEM((cells * GROUP, CHAN), jnp.bfloat16),
            pltpu.VMEM((cells * GROUP + 2 * GROUP, MID), jnp.float32),
            pltpu.VMEM((cells * GROUP + 2 * EDGE, 3 * MID), jnp.bfloat16),
        ],
    )
    flops = 2 * slots * cells * (BLOCKS * (2 * CHAN * MID + 9 * MID * MID) + CHAN * emb)
    return pl.pallas_call(
        cell_kernel,
        grid_spec=grid_spec,
        out_shape=jax.ShapeDtypeStruct((cells, slots, emb), jnp.float32),
        compiler_params=pltpu.CompilerParams(
            dimension_semantics=("arbitrary",), vmem_limit_bytes=60 * 1024 * 1024
        ),
        cost_estimate=pl.CostEstimate(
            flops=flops, transcendentals=0, bytes_accessed=slots * cells * (2 * CHAN + 4 * emb + 4)
        ),
    )(count, xt, weight, w_reduce, b_reduce, ws, b_spatial, w_expand, proj_w)


def grid_box_kernel(w_ref, hu_ref, hd_ref, o_ref, v_ref, ub_ref, db_ref, sh_ref):
    slots = w_ref.shape[2]
    ub_ref[:, 8 : 8 + slots, :] = w_ref[TILE - 1]
    ub_ref[:, 4:8, :] = hu_ref[...]
    db_ref[:, 0:slots, :] = w_ref[0]
    db_ref[:, slots : slots + 4, :] = hd_ref[...]
    v_ref[0] = ub_ref[:, 4 : 4 + slots, :] + w_ref[0] + w_ref[1]
    v_ref[TILE - 1] = w_ref[TILE - 2] + w_ref[TILE - 1] + db_ref[:, 4 : 4 + slots, :]

    def vertical(i, carry):
        v_ref[i] = w_ref[i - 1] + w_ref[i] + w_ref[i + 1]
        return carry

    lax.fori_loop(1, TILE - 1, vertical, 0)
    slot = lax.broadcasted_iota(jnp.int32, (slots, w_ref.shape[3]), 0) & (TCOLS - 1)

    def horizontal(i, carry):
        o_ref[i, 1 : TILE - 1] = (
            v_ref[i, 0 : TILE - 2] + v_ref[i, 1 : TILE - 1] + v_ref[i, 2:TILE]
        ) / 9.0
        sh_ref[8 : 8 + slots, :] = v_ref[i, TILE - 1]
        left = jnp.where(slot != 0, sh_ref[7 : 7 + slots, :], 0.0)
        o_ref[i, 0] = (left + v_ref[i, 0] + v_ref[i, 1]) / 9.0
        sh_ref[8 : 8 + slots, :] = v_ref[i, 0]
        right = jnp.where(slot != TCOLS - 1, sh_ref[9 : 9 + slots, :], 0.0)
        o_ref[i, TILE - 1] = (v_ref[i, TILE - 2] + v_ref[i, TILE - 1] + right) / 9.0
        return carry

    lax.fori_loop(0, TILE, horizontal, 0)


def grid_box_average(w, up, down):
    cells, slots, emb = w.shape
    w4 = w.reshape(TILE, TILE, slots, emb)
    out = pl.pallas_call(
        grid_box_kernel,
        out_shape=jax.ShapeDtypeStruct(w4.shape, jnp.float32),
        scratch_shapes=[
            pltpu.VMEM(w4.shape, jnp.float32),
            pltpu.VMEM((TILE, slots + 8, emb), jnp.float32),
            pltpu.VMEM((TILE, slots + 8, emb), jnp.float32),
            pltpu.VMEM((slots + 16, emb), jnp.float32),
        ],
        compiler_params=pltpu.CompilerParams(vmem_limit_bytes=48 * 1024 * 1024),
        cost_estimate=pl.CostEstimate(
            flops=10 * slots * cells * emb, transcendentals=0, bytes_accessed=8 * slots * cells * emb
        ),
    )(w4, up, down)
    return out.reshape(cells, slots, emb)


def row_box(halo):
    before = jnp.concatenate(
        [jnp.pad(halo[TILE - 1 :, :-1], ((0, 0), (1, 0), (0, 0))), halo[:-1]], axis=0
    )
    after = jnp.concatenate([halo[1:], jnp.pad(halo[:1, 1:], ((0, 0), (0, 1), (0, 0)))], axis=0)
    return (before + halo + after) / 9.0


def fix_kernel(a_ref, hu_ref, hd_ref, o_ref):
    g = pl.program_id(0)
    slots = a_ref.shape[2]
    o_ref[...] = a_ref[...]

    @pl.when(g == 0)
    def _():
        o_ref[0, :, 0:TCOLS, :] = a_ref[0, :, 0:TCOLS, :] + hu_ref[...]

    @pl.when(g == 1)
    def _():
        o_ref[0, :, slots - TCOLS :, :] = a_ref[0, :, slots - TCOLS :, :] + hd_ref[...]


def add_halo_rows(averaged, up, down):
    cells, slots, emb = averaged.shape
    a4 = averaged.reshape(TILE, TILE, slots, emb)
    row = pl.BlockSpec((1, TILE, slots, emb), lambda g: (g * (TILE - 1), 0, 0, 0))
    out = pl.pallas_call(
        fix_kernel,
        grid=(2,),
        in_specs=[row, pl.BlockSpec(up.shape, lambda g: (0, 0, 0)), pl.BlockSpec(down.shape, lambda g: (0, 0, 0))],
        out_specs=row,
        out_shape=jax.ShapeDtypeStruct(a4.shape, jnp.float32),
        input_output_aliases={0: 0},
    )(a4, up, down)
    return out.reshape(cells, slots, emb)


def per_device(
    tiles, counts, tissue_mask, w_reduce, b_reduce, w_spatial, b_spatial, w_expand, proj_w
):
    slots = tiles.shape[2]
    held = counts[0]
    positions = jnp.arange(slots, dtype=jnp.int32)
    alive = positions < held[0]
    weight = jnp.where(alive[:, None], tissue_mask[0, 0], 0).astype(jnp.float32)
    computed = cell_features(
        held,
        jnp.transpose(tiles[0, 0], (1, 0, 2)),
        weight.T[:, :, None].astype(jnp.bfloat16),
        w_reduce,
        b_reduce,
        w_spatial,
        b_spatial,
        w_expand,
        proj_w,
    )
    count = lax.axis_size("region")
    forward = [(i, i + 1) for i in range(count - 1)]
    backward = [(target, source) for source, target in forward]
    up = lax.ppermute(computed[CELLS - TILE :, slots - TCOLS :], "region", forward)
    down = lax.ppermute(computed[:TILE, :TCOLS], "region", backward)
    none = jnp.zeros(up.shape, up.dtype)
    averaged = grid_box_average(computed, none, none)
    averaged = add_halo_rows(averaged, row_box(up), row_box(down))
    return jnp.transpose(averaged, (1, 0, 2)).reshape(1, 1, slots, CELLS, -1)


def solution(mesh):
    placed = (
        P("slide", "region", None, None, None),
        P("slide", "region"),
        P("slide", "region", None, None),
        P(),
        P(),
        P(),
        P(),
        P(),
        P(),
    )
    return jax.shard_map(
        per_device,
        mesh=mesh,
        in_specs=placed,
        out_specs=P("slide", "region", None, None, None),
        check_vma=False,
    )
```

```python
import jax
import jax.numpy as jnp
from jax import lax
from jax.experimental import pallas as pl
from jax.experimental.pallas import tpu as pltpu
from jax.sharding import PartitionSpec as P

CHAN = 1024
MID = 256
TILE = 14
BLOCKS = 2
TCOLS = 4
CELLS = TILE * TILE
WIDE = 16
PADDED = TILE * WIDE


GROUP = 16
SPAN = 7 * TILE
ROWS = SPAN * GROUP
EDGE = TILE * GROUP


def cell_kernel(
    count_ref, x_ref, m_ref, wr_ref, br_ref, ws_ref, bs_ref, we_ref, pw_ref, o_ref, hu_ref, hd_ref,
    cur_ref, r_ref, c_ref,
):
    g = pl.program_id(0)
    total = CELLS * GROUP
    chunks = CELLS // SPAN

    last = pl.num_programs(0) - 1
    cells = o_ref.shape[0]

    @pl.when(g * GROUP >= count_ref[0])
    def _():
        o_ref[...] = jnp.zeros(o_ref.shape, o_ref.dtype)

        @pl.when(g == last)
        def _():
            hu_ref[...] = jnp.zeros(hu_ref.shape, hu_ref.dtype)

        @pl.when(g == 0)
        def _():
            hd_ref[...] = jnp.zeros(hd_ref.shape, hd_ref.dtype)

    @pl.when(g * GROUP < count_ref[0])
    def _():
        r_ref[0:GROUP, :] = jnp.zeros((GROUP, MID), jnp.float32)
        r_ref[GROUP + total :, :] = jnp.zeros((GROUP, MID), jnp.float32)
        c_ref[0:EDGE, :] = jnp.zeros((EDGE, 3 * MID), jnp.bfloat16)
        c_ref[EDGE + total :, :] = jnp.zeros((EDGE, 3 * MID), jnp.bfloat16)
        lane = lax.broadcasted_iota(jnp.int32, (SPAN, GROUP, MID), 0)
        keep_left = lane != 0
        keep_right = lane != TILE - 1
        for row in range(1, SPAN // TILE):
            keep_left = keep_left & (lane != TILE * row)
            keep_right = keep_right & (lane != TILE * row + TILE - 1)

        def source(b, q0):
            if b == 0:
                return x_ref[pl.ds(q0 // GROUP, SPAN)].reshape(ROWS, CHAN)
            return cur_ref[pl.ds(q0, ROWS), :]

        for b in range(BLOCKS):
            for ch in range(chunks):
                q0 = ch * ROWS
                r = jnp.dot(source(b, q0), wr_ref[b], preferred_element_type=jnp.float32)
                r_ref[pl.ds(GROUP + q0, ROWS), :] = jnp.maximum(r + br_ref[b : b + 1, :], 0.0)
            for ch in range(chunks):
                q0 = ch * ROWS
                left = r_ref[pl.ds(q0, ROWS), :].reshape(SPAN, GROUP, MID)
                centre = r_ref[pl.ds(GROUP + q0, ROWS), :]
                right = r_ref[pl.ds(2 * GROUP + q0, ROWS), :].reshape(SPAN, GROUP, MID)
                left = jnp.where(keep_left, left, 0.0).reshape(ROWS, MID)
                right = jnp.where(keep_right, right, 0.0).reshape(ROWS, MID)
                c_ref[pl.ds(EDGE + q0, ROWS), 0:MID] = left.astype(jnp.bfloat16)
                c_ref[pl.ds(EDGE + q0, ROWS), MID : 2 * MID] = centre.astype(jnp.bfloat16)
                c_ref[pl.ds(EDGE + q0, ROWS), 2 * MID :] = right.astype(jnp.bfloat16)
            for ch in range(chunks):
                q0 = ch * ROWS
                acc = jnp.dot(c_ref[pl.ds(q0, ROWS), :], ws_ref[b, 0], preferred_element_type=jnp.float32)
                acc += jnp.dot(c_ref[pl.ds(EDGE + q0, ROWS), :], ws_ref[b, 1], preferred_element_type=jnp.float32)
                acc += jnp.dot(c_ref[pl.ds(2 * EDGE + q0, ROWS), :], ws_ref[b, 2], preferred_element_type=jnp.float32)
                spatial = jnp.maximum(acc + bs_ref[b : b + 1, :], 0.0).astype(jnp.bfloat16)
                e = jnp.dot(spatial, we_ref[b], preferred_element_type=jnp.float32)
                res = source(b, q0).astype(jnp.float32)
                cur_ref[pl.ds(q0, ROWS), :] = jnp.maximum(res + e, 0.0).astype(jnp.bfloat16)
        for ch in range(chunks):
            q0 = ch * ROWS
            proj = jnp.dot(cur_ref[pl.ds(q0, ROWS), :], pw_ref[...], preferred_element_type=jnp.float32)
            c0 = ch * SPAN
            o_ref[pl.ds(c0, SPAN)] = proj.reshape(SPAN, GROUP, -1) * m_ref[pl.ds(c0, SPAN)]

        @pl.when(g == last)
        def _():
            hu_ref[...] = o_ref[cells - TILE :, GROUP - TCOLS :, :]

        @pl.when(g == 0)
        def _():
            hd_ref[...] = o_ref[0:TILE, 0:TCOLS, :]


def cell_features(count, xt, weight, w_reduce, b_reduce, w_spatial, b_spatial, w_expand, proj_w):
    cells, slots, _ = xt.shape
    emb = proj_w.shape[1]
    ws = w_spatial.reshape(BLOCKS, 3, 3 * MID, MID)
    def live(g, c):
        return (0, jnp.maximum(jnp.minimum(g, (c[0] - 1) // GROUP), 0), 0)

    def whole(nd):
        return lambda g, c: (0,) * nd

    once = pl.Buffered(1)
    grid_spec = pltpu.PrefetchScalarGridSpec(
        num_scalar_prefetch=1,
        grid=(slots // GROUP,),
        in_specs=[
            pl.BlockSpec((cells, GROUP, CHAN), live),
            pl.BlockSpec((cells, GROUP, 1), lambda g, c: (0, g, 0)),
            pl.BlockSpec((BLOCKS, CHAN, MID), whole(3), pipeline_mode=once),
            pl.BlockSpec((BLOCKS, MID), whole(2), pipeline_mode=once),
            pl.BlockSpec((BLOCKS, 3, 3 * MID, MID), whole(4), pipeline_mode=once),
            pl.BlockSpec((BLOCKS, MID), whole(2), pipeline_mode=once),
            pl.BlockSpec((BLOCKS, MID, CHAN), whole(3), pipeline_mode=once),
            pl.BlockSpec((CHAN, emb), whole(2), pipeline_mode=once),
        ],
        out_specs=[
            pl.BlockSpec((cells, GROUP, emb), lambda g, c: (0, g, 0)),
            pl.BlockSpec((TILE, TCOLS, emb), lambda g, c: (0, 0, 0)),
            pl.BlockSpec((TILE, TCOLS, emb), lambda g, c: (0, 0, 0)),
        ],
        scratch_shapes=[
            pltpu.VMEM((cells * GROUP, CHAN), jnp.bfloat16),
            pltpu.VMEM((cells * GROUP + 2 * GROUP, MID), jnp.float32),
            pltpu.VMEM((cells * GROUP + 2 * EDGE, 3 * MID), jnp.bfloat16),
        ],
    )
    flops = 2 * slots * cells * (BLOCKS * (2 * CHAN * MID + 9 * MID * MID) + CHAN * emb)
    return pl.pallas_call(
        cell_kernel,
        grid_spec=grid_spec,
        out_shape=[
            jax.ShapeDtypeStruct((cells, slots, emb), jnp.float32),
            jax.ShapeDtypeStruct((TILE, TCOLS, emb), jnp.float32),
            jax.ShapeDtypeStruct((TILE, TCOLS, emb), jnp.float32),
        ],
        compiler_params=pltpu.CompilerParams(
            dimension_semantics=("arbitrary",), vmem_limit_bytes=60 * 1024 * 1024
        ),
        cost_estimate=pl.CostEstimate(
            flops=flops, transcendentals=0, bytes_accessed=slots * cells * (2 * CHAN + 4 * emb + 4)
        ),
    )(count, xt, weight, w_reduce, b_reduce, ws, b_spatial, w_expand, proj_w)


def grid_box_kernel(w_ref, hu_ref, hd_ref, o_ref, v_ref, ub_ref, db_ref, sh_ref):
    slots = w_ref.shape[2]
    ub_ref[:, 8 : 8 + slots, :] = w_ref[TILE - 1]
    ub_ref[:, 4:8, :] = hu_ref[...]
    db_ref[:, 0:slots, :] = w_ref[0]
    db_ref[:, slots : slots + 4, :] = hd_ref[...]
    v_ref[0] = ub_ref[:, 4 : 4 + slots, :] + w_ref[0] + w_ref[1]
    v_ref[TILE - 1] = w_ref[TILE - 2] + w_ref[TILE - 1] + db_ref[:, 4 : 4 + slots, :]

    def vertical(i, carry):
        v_ref[i] = w_ref[i - 1] + w_ref[i] + w_ref[i + 1]
        return carry

    lax.fori_loop(1, TILE - 1, vertical, 0)
    slot = lax.broadcasted_iota(jnp.int32, (slots, w_ref.shape[3]), 0) & (TCOLS - 1)

    def horizontal(i, carry):
        o_ref[i, 1 : TILE - 1] = (
            v_ref[i, 0 : TILE - 2] + v_ref[i, 1 : TILE - 1] + v_ref[i, 2:TILE]
        ) / 9.0
        sh_ref[8 : 8 + slots, :] = v_ref[i, TILE - 1]
        left = jnp.where(slot != 0, sh_ref[7 : 7 + slots, :], 0.0)
        o_ref[i, 0] = (left + v_ref[i, 0] + v_ref[i, 1]) / 9.0
        sh_ref[8 : 8 + slots, :] = v_ref[i, 0]
        right = jnp.where(slot != TCOLS - 1, sh_ref[9 : 9 + slots, :], 0.0)
        o_ref[i, TILE - 1] = (v_ref[i, TILE - 2] + v_ref[i, TILE - 1] + right) / 9.0
        return carry

    lax.fori_loop(0, TILE, horizontal, 0)


def grid_box_average(w, up, down):
    cells, slots, emb = w.shape
    w4 = w.reshape(TILE, TILE, slots, emb)
    out = pl.pallas_call(
        grid_box_kernel,
        out_shape=jax.ShapeDtypeStruct(w4.shape, jnp.float32),
        scratch_shapes=[
            pltpu.VMEM(w4.shape, jnp.float32),
            pltpu.VMEM((TILE, slots + 8, emb), jnp.float32),
            pltpu.VMEM((TILE, slots + 8, emb), jnp.float32),
            pltpu.VMEM((slots + 16, emb), jnp.float32),
        ],
        compiler_params=pltpu.CompilerParams(vmem_limit_bytes=48 * 1024 * 1024),
        cost_estimate=pl.CostEstimate(
            flops=10 * slots * cells * emb, transcendentals=0, bytes_accessed=8 * slots * cells * emb
        ),
    )(w4, up, down)
    return out.reshape(cells, slots, emb)


def per_device(
    tiles, counts, tissue_mask, w_reduce, b_reduce, w_spatial, b_spatial, w_expand, proj_w
):
    slots = tiles.shape[2]
    held = counts[0]
    positions = jnp.arange(slots, dtype=jnp.int32)
    alive = positions < held[0]
    weight = jnp.where(alive[:, None], tissue_mask[0, 0], 0).astype(jnp.float32)
    computed, last_row, first_row = cell_features(
        held,
        jnp.transpose(tiles[0, 0], (1, 0, 2)),
        weight.T[:, :, None].astype(jnp.bfloat16),
        w_reduce,
        b_reduce,
        w_spatial,
        b_spatial,
        w_expand,
        proj_w,
    )
    count = lax.axis_size("region")
    forward = [(i, i + 1) for i in range(count - 1)]
    backward = [(target, source) for source, target in forward]
    up = lax.ppermute(last_row, "region", forward)
    down = lax.ppermute(first_row, "region", backward)
    averaged = grid_box_average(computed, up, down)
    return jnp.transpose(averaged, (1, 0, 2)).reshape(1, 1, slots, CELLS, -1)


def solution(mesh):
    placed = (
        P("slide", "region", None, None, None),
        P("slide", "region"),
        P("slide", "region", None, None),
        P(),
        P(),
        P(),
        P(),
        P(),
        P(),
    )
    return jax.shard_map(
        per_device,
        mesh=mesh,
        in_specs=placed,
        out_specs=P("slide", "region", None, None, None),
        check_vma=False,
    )
```

```python
import jax
import jax.numpy as jnp
from jax import lax
from jax.experimental import pallas as pl
from jax.experimental.pallas import tpu as pltpu
from jax.sharding import PartitionSpec as P

CHAN = 1024
MID = 256
TILE = 14
BLOCKS = 2
TCOLS = 4
CELLS = TILE * TILE
WIDE = 16
PADDED = TILE * WIDE


GROUP = 16
SPAN = 7 * TILE
ROWS = SPAN * GROUP
EDGE = TILE * GROUP


def cell_kernel(
    count_ref, x_ref, m_ref, wr_ref, br_ref, ws_ref, bs_ref, we_ref, pw_ref, o_ref,
    cur_ref, r_ref, c_ref,
):
    g = pl.program_id(0)
    total = CELLS * GROUP
    chunks = CELLS // SPAN

    @pl.when(g * GROUP >= count_ref[0])
    def _():
        o_ref[...] = jnp.zeros(o_ref.shape, o_ref.dtype)

    @pl.when(g * GROUP < count_ref[0])
    def _():
        r_ref[0:GROUP, :] = jnp.zeros((GROUP, MID), jnp.float32)
        r_ref[GROUP + total :, :] = jnp.zeros((GROUP, MID), jnp.float32)
        c_ref[0:EDGE, :] = jnp.zeros((EDGE, 3 * MID), jnp.bfloat16)
        c_ref[EDGE + total :, :] = jnp.zeros((EDGE, 3 * MID), jnp.bfloat16)
        lane = lax.broadcasted_iota(jnp.int32, (SPAN, GROUP, MID), 0)
        keep_left = lane != 0
        keep_right = lane != TILE - 1
        for row in range(1, SPAN // TILE):
            keep_left = keep_left & (lane != TILE * row)
            keep_right = keep_right & (lane != TILE * row + TILE - 1)

        def source(b, q0):
            if b == 0:
                return x_ref[pl.ds(q0 // GROUP, SPAN)].reshape(ROWS, CHAN)
            return cur_ref[pl.ds(q0, ROWS), :]

        for b in range(BLOCKS):
            for ch in range(chunks):
                q0 = ch * ROWS
                r = jnp.dot(source(b, q0), wr_ref[b], preferred_element_type=jnp.float32)
                r_ref[pl.ds(GROUP + q0, ROWS), :] = jnp.maximum(r + br_ref[b : b + 1, :], 0.0)
            for ch in range(chunks):
                q0 = ch * ROWS
                left = r_ref[pl.ds(q0, ROWS), :].reshape(SPAN, GROUP, MID)
                centre = r_ref[pl.ds(GROUP + q0, ROWS), :]
                right = r_ref[pl.ds(2 * GROUP + q0, ROWS), :].reshape(SPAN, GROUP, MID)
                left = jnp.where(keep_left, left, 0.0).reshape(ROWS, MID)
                right = jnp.where(keep_right, right, 0.0).reshape(ROWS, MID)
                c_ref[pl.ds(EDGE + q0, ROWS), 0:MID] = left.astype(jnp.bfloat16)
                c_ref[pl.ds(EDGE + q0, ROWS), MID : 2 * MID] = centre.astype(jnp.bfloat16)
                c_ref[pl.ds(EDGE + q0, ROWS), 2 * MID :] = right.astype(jnp.bfloat16)
            for ch in range(chunks):
                q0 = ch * ROWS
                acc = jnp.dot(c_ref[pl.ds(q0, ROWS), :], ws_ref[b, 0], preferred_element_type=jnp.float32)
                acc += jnp.dot(c_ref[pl.ds(EDGE + q0, ROWS), :], ws_ref[b, 1], preferred_element_type=jnp.float32)
                acc += jnp.dot(c_ref[pl.ds(2 * EDGE + q0, ROWS), :], ws_ref[b, 2], preferred_element_type=jnp.float32)
                spatial = jnp.maximum(acc + bs_ref[b : b + 1, :], 0.0).astype(jnp.bfloat16)
                e = jnp.dot(spatial, we_ref[b], preferred_element_type=jnp.float32)
                res = source(b, q0).astype(jnp.float32)
                cur_ref[pl.ds(q0, ROWS), :] = jnp.maximum(res + e, 0.0).astype(jnp.bfloat16)
        for ch in range(chunks):
            q0 = ch * ROWS
            proj = jnp.dot(cur_ref[pl.ds(q0, ROWS), :], pw_ref[...], preferred_element_type=jnp.float32)
            c0 = ch * SPAN
            o_ref[pl.ds(c0, SPAN)] = proj.reshape(SPAN, GROUP, -1) * m_ref[pl.ds(c0, SPAN)].astype(jnp.float32)


def cell_features(count, xt, weight, w_reduce, b_reduce, w_spatial, b_spatial, w_expand, proj_w):
    cells, slots, _ = xt.shape
    emb = proj_w.shape[1]
    ws = w_spatial.reshape(BLOCKS, 3, 3 * MID, MID)
    def live(g, c):
        return (0, jnp.maximum(jnp.minimum(g, (c[0] - 1) // GROUP), 0), 0)

    def whole(nd):
        return lambda g, c: (0,) * nd

    once = pl.Buffered(1)
    grid_spec = pltpu.PrefetchScalarGridSpec(
        num_scalar_prefetch=1,
        grid=(slots // GROUP,),
        in_specs=[
            pl.BlockSpec((cells, GROUP, CHAN), live),
            pl.BlockSpec((cells, GROUP, 1), lambda g, c: (0, g, 0)),
            pl.BlockSpec((BLOCKS, CHAN, MID), whole(3), pipeline_mode=once),
            pl.BlockSpec((BLOCKS, MID), whole(2), pipeline_mode=once),
            pl.BlockSpec((BLOCKS, 3, 3 * MID, MID), whole(4), pipeline_mode=once),
            pl.BlockSpec((BLOCKS, MID), whole(2), pipeline_mode=once),
            pl.BlockSpec((BLOCKS, MID, CHAN), whole(3), pipeline_mode=once),
            pl.BlockSpec((CHAN, emb), whole(2), pipeline_mode=once),
        ],
        out_specs=pl.BlockSpec((cells, GROUP, emb), lambda g, c: (0, g, 0)),
        scratch_shapes=[
            pltpu.VMEM((cells * GROUP, CHAN), jnp.bfloat16),
            pltpu.VMEM((cells * GROUP + 2 * GROUP, MID), jnp.float32),
            pltpu.VMEM((cells * GROUP + 2 * EDGE, 3 * MID), jnp.bfloat16),
        ],
    )
    flops = 2 * slots * cells * (BLOCKS * (2 * CHAN * MID + 9 * MID * MID) + CHAN * emb)
    return pl.pallas_call(
        cell_kernel,
        grid_spec=grid_spec,
        out_shape=jax.ShapeDtypeStruct((cells, slots, emb), jnp.float32),
        compiler_params=pltpu.CompilerParams(
            dimension_semantics=("arbitrary",), vmem_limit_bytes=60 * 1024 * 1024
        ),
        cost_estimate=pl.CostEstimate(
            flops=flops, transcendentals=0, bytes_accessed=slots * cells * (2 * CHAN + 4 * emb + 4)
        ),
    )(count, xt, weight, w_reduce, b_reduce, ws, b_spatial, w_expand, proj_w)


def grid_box_kernel(w_ref, hu_ref, hd_ref, o_ref, v_ref, ub_ref, db_ref, sh_ref):
    slots = w_ref.shape[2]
    ub_ref[:, 8 : 8 + slots, :] = w_ref[TILE - 1]
    ub_ref[:, 4:8, :] = hu_ref[...]
    db_ref[:, 0:slots, :] = w_ref[0]
    db_ref[:, slots : slots + 4, :] = hd_ref[...]
    v_ref[0] = ub_ref[:, 4 : 4 + slots, :] + w_ref[0] + w_ref[1]
    v_ref[TILE - 1] = w_ref[TILE - 2] + w_ref[TILE - 1] + db_ref[:, 4 : 4 + slots, :]

    def vertical(i, carry):
        v_ref[i] = w_ref[i - 1] + w_ref[i] + w_ref[i + 1]
        return carry

    lax.fori_loop(1, TILE - 1, vertical, 0)
    slot = lax.broadcasted_iota(jnp.int32, (slots, w_ref.shape[3]), 0) & (TCOLS - 1)

    def horizontal(i, carry):
        o_ref[i, 1 : TILE - 1] = (
            v_ref[i, 0 : TILE - 2] + v_ref[i, 1 : TILE - 1] + v_ref[i, 2:TILE]
        ) / 9.0
        sh_ref[8 : 8 + slots, :] = v_ref[i, TILE - 1]
        left = jnp.where(slot != 0, sh_ref[7 : 7 + slots, :], 0.0)
        o_ref[i, 0] = (left + v_ref[i, 0] + v_ref[i, 1]) / 9.0
        sh_ref[8 : 8 + slots, :] = v_ref[i, 0]
        right = jnp.where(slot != TCOLS - 1, sh_ref[9 : 9 + slots, :], 0.0)
        o_ref[i, TILE - 1] = (v_ref[i, TILE - 2] + v_ref[i, TILE - 1] + right) / 9.0
        return carry

    lax.fori_loop(0, TILE, horizontal, 0)


def grid_box_average(w, up, down):
    cells, slots, emb = w.shape
    w4 = w.reshape(TILE, TILE, slots, emb)
    out = pl.pallas_call(
        grid_box_kernel,
        out_shape=jax.ShapeDtypeStruct(w4.shape, jnp.float32),
        scratch_shapes=[
            pltpu.VMEM(w4.shape, jnp.float32),
            pltpu.VMEM((TILE, slots + 8, emb), jnp.float32),
            pltpu.VMEM((TILE, slots + 8, emb), jnp.float32),
            pltpu.VMEM((slots + 16, emb), jnp.float32),
        ],
        compiler_params=pltpu.CompilerParams(vmem_limit_bytes=48 * 1024 * 1024),
        cost_estimate=pl.CostEstimate(
            flops=10 * slots * cells * emb, transcendentals=0, bytes_accessed=8 * slots * cells * emb
        ),
    )(w4, up, down)
    return out.reshape(cells, slots, emb)


def per_device(
    tiles, counts, tissue_mask, w_reduce, b_reduce, w_spatial, b_spatial, w_expand, proj_w
):
    slots = tiles.shape[2]
    held = counts[0]
    positions = jnp.arange(slots, dtype=jnp.int32)
    alive = positions < held[0]
    weight = jnp.where(alive[:, None], tissue_mask[0, 0], 0).astype(jnp.float32)
    computed = cell_features(
        held,
        jnp.transpose(tiles[0, 0], (1, 0, 2)),
        weight.T[:, :, None].astype(jnp.int8),
        w_reduce,
        b_reduce,
        w_spatial,
        b_spatial,
        w_expand,
        proj_w,
    )
    count = lax.axis_size("region")
    forward = [(i, i + 1) for i in range(count - 1)]
    backward = [(target, source) for source, target in forward]
    up = lax.ppermute(computed[CELLS - TILE :, slots - TCOLS :], "region", forward)
    down = lax.ppermute(computed[:TILE, :TCOLS], "region", backward)
    averaged = grid_box_average(computed, up, down)
    return jnp.transpose(averaged, (1, 0, 2)).reshape(1, 1, slots, CELLS, -1)


def solution(mesh):
    placed = (
        P("slide", "region", None, None, None),
        P("slide", "region"),
        P("slide", "region", None, None),
        P(),
        P(),
        P(),
        P(),
        P(),
        P(),
    )
    return jax.shard_map(
        per_device,
        mesh=mesh,
        in_specs=placed,
        out_specs=P("slide", "region", None, None, None),
        check_vma=False,
    )
```
